256 devices in a mesh: gx: 16 (over y, x), gy: 16 (over z, core).
Axes of the slice: x: 4, y: 4, z: 8, core: 2. Of those that a mesh axis runs over, the one named last changes fastest.
Arguments:
- spatial_factor: float32 [64, 256, 32, 64], P('gx', 'gy'), may hold values from -60 to 60
- coupling: float32 [64, 64], replicated, may hold values from -1 to 5
- orient_factor: float32 [2048, 64], replicated, may hold values from -6 to 6
- directions: float32 [3, 2048], replicated, may hold values from -1 to 1, as said below
Outputs:
- new_spatial: float32 [64, 256, 32, 64], P('gx', 'gy')
- new_coupling: float32 [64, 64], replicated
- new_orient: float32 [2048, 64], replicated
The draws below stay inside these ranges and needn't reach their ends.
Inputs may be any that keep to these rules, and one draw needn't show every extreme that they name: `directions`: each column is a unit vector.
All inputs are finite; a program needn't handle non-finite values.
Results may differ from the reference program's by a relative error of at most 0.0003.
Values sent between devices are 32-bit elements; how exact they have to be, the bound alone decides.
A program may use at most 64 MiB of HBM per device.

```python
import math
import jax
import jax.numpy as jnp
from jax import lax

R = 64
NO = 2048
STEPS = 2
NX = 64
NY = 256
NZ = 32


def draw_spatial_factor(key, part):
    across = jnp.arange(NX, dtype=jnp.float32)[:, None, None, None] / NX
    along = jnp.arange(NY, dtype=jnp.float32)[None, :, None, None] / NY
    base = jnp.clip(jax.random.normal(key, (NX, NY, NZ, R), jnp.float32), -6.0, 6.0)
    growth = across + along
    return base * jnp.exp(math.log(3.0) * growth)


def draw_coupling(key, part):
    first_key, second_key = jax.random.split(jax.random.fold_in(key, 11))
    diagonal = jnp.exp(jax.random.uniform(first_key, (R,), jnp.float32, math.log(2.0), math.log(4.0)))
    others = jnp.clip(jax.random.normal(second_key, (R, R), jnp.float32), -3.0, 3.0)
    identity = jnp.eye(R, dtype=jnp.float32)
    return others * (0.7 / math.sqrt(R)) * (1.0 - identity) + identity * diagonal[None, :]


def draw_directions(key, part):
    first_key, second_key = jax.random.split(jax.random.fold_in(key, 23))
    height = jax.random.uniform(first_key, (NO,), jnp.float32, -1.0, 1.0)
    azimuth = jax.random.uniform(second_key, (NO,), jnp.float32, -math.pi, math.pi)
    radius = jnp.sqrt(jnp.maximum(1.0 - height * height, 0.0))
    return jnp.stack([radius * jnp.cos(azimuth), radius * jnp.sin(azimuth), height])


def centred(stream_key, shape, width, limit, kind=jnp.bfloat16):
    array = jax.random.normal(stream_key, shape, jnp.float32) * width
    return jnp.minimum(jnp.maximum(array, -limit), limit).astype(kind)


def setup_inputs(seed: int = 0) -> dict:
    splits = jax.random.split(jax.random.key(seed), 5)
    spatial_factor = draw_spatial_factor(jax.random.fold_in(splits[4], 71), 0)
    coupling = draw_coupling(jax.random.fold_in(splits[4], 71), 0)
    orient_factor = centred(splits[2], (NO, R), 1.0, 6.0, jnp.float32)
    directions = draw_directions(jax.random.fold_in(splits[4], 71), 0)
    return {"spatial_factor": spatial_factor, "coupling": coupling, "orient_factor": orient_factor, "directions": directions}


courant = 0.3
tumble = 0.2
highest = lax.Precision.HIGHEST

def matmul(left, right):
    return jnp.matmul(left, right, precision=highest)

def motility(density):
    return 1.0 / (1.0 + density * density)

def orient_tables(orient, directions):
    e_plus = jnp.maximum(directions, 0.0)
    e_minus = jnp.maximum(-directions, 0.0)
    orient_count = orient.shape[0]
    c_plus = [matmul((orient * e_plus[dim_index][:, None]).T, orient) / orient_count for dim_index in range(3)]
    c_minus = [matmul((orient * e_minus[dim_index][:, None]).T, orient) / orient_count for dim_index in range(3)]
    mean_row = jnp.mean(orient, axis=0)
    return (e_plus, e_minus, c_plus, c_minus, mean_row)

def differences(padded):
    center = padded[1:-1, 1:-1]
    backward = [center - padded[:-2, 1:-1], center - padded[1:-1, :-2], center - jnp.roll(center, 1, 2)]
    forward = [padded[2:, 1:-1] - center, padded[1:-1, 2:] - center, jnp.roll(center, -1, 2) - center]
    return (backward, forward)

def drift_term(flux_ext, c_plus, c_minus):
    backward, forward = differences(flux_ext)
    summed = jnp.zeros(backward[0].shape, jnp.float32)
    for dim_index in range(3):
        summed = summed + matmul(backward[dim_index], c_plus[dim_index]) - matmul(forward[dim_index], c_minus[dim_index])
    return summed

def k_update(k_center, rho_center, flux_ext, c_plus, c_minus, mean_row):
    return k_center - courant * drift_term(flux_ext, c_plus, c_minus) + tumble * (rho_center[..., None] * mean_row - k_center)

def projections(base, speed_ext):
    rank_width = base.shape[-1]
    rows_flat = base.reshape(-1, rank_width)
    backward, forward = differences(speed_ext)
    return jnp.stack([matmul(rows_flat.T, member.reshape(-1, rank_width)) for member in backward + forward])

def orient_update(start_coupling, orient, galerkin, e_plus, e_minus, c_plus, c_minus, mean_row):
    mid_coupling = start_coupling - tumble * (jnp.outer(matmul(start_coupling, mean_row), mean_row) - start_coupling)
    for dim_index in range(3):
        mid_coupling = mid_coupling + courant * (matmul(matmul(galerkin[dim_index], start_coupling), c_plus[dim_index]) - matmul(matmul(galerkin[dim_index + 3], start_coupling), c_minus[dim_index]))
    l_matrix = matmul(orient, mid_coupling.T)
    l_next = l_matrix + tumble * (jnp.mean(l_matrix, axis=0)[None, :] - l_matrix)
    for dim_index in range(3):
        l_next = l_next - courant * (e_plus[dim_index][:, None] * matmul(l_matrix, galerkin[dim_index].T) - e_minus[dim_index][:, None] * matmul(l_matrix, galerkin[dim_index + 3].T))
    chol_lower = jnp.linalg.cholesky(matmul(l_next.T, l_next) / l_next.shape[0])
    new_orient = lax.linalg.triangular_solve(chol_lower, l_next, left_side=False, lower=True, transpose_a=True)
    return (chol_lower, new_orient)

def wrap_pad(field):
    return jnp.pad(field, ((1, 1), (1, 1), (0, 0), (0, 0)), mode='wrap')

def reference(spatial_factor, coupling, orient_factor, directions):
    spatial = spatial_factor
    orient = orient_factor
    rank_width = spatial.shape[-1]
    cell_count = NX * NY * NZ
    for step_index in range(STEPS):
        e_plus, e_minus, c_plus, c_minus, mean_row = orient_tables(orient, directions)
        k_matrix = matmul(spatial, coupling)
        density = matmul(k_matrix, mean_row)
        flux_ext = wrap_pad(motility(density)[..., None] * k_matrix)
        k_next = k_update(k_matrix, density, flux_ext, c_plus, c_minus, mean_row)
        rows_flat = k_next.reshape(-1, rank_width)
        chol_lower = jnp.linalg.cholesky(matmul(rows_flat.T, rows_flat) / cell_count)
        new_spatial = lax.linalg.triangular_solve(chol_lower, rows_flat, left_side=False, lower=True, transpose_a=True).reshape(k_next.shape)
        speed_ext = wrap_pad(motility(matmul(k_next, mean_row))[..., None] * new_spatial)
        galerkin = projections(new_spatial, speed_ext) / cell_count
        coupling, orient = orient_update(chol_lower.T, orient, galerkin, e_plus, e_minus, c_plus, c_minus, mean_row)
        spatial = new_spatial
    return (spatial, coupling, orient)
```

```python
import functools

import jax
import jax.numpy as jnp
from jax import lax
from jax.experimental import pallas as pl
from jax.experimental.pallas import tpu as pltpu
from jax.sharding import PartitionSpec as P

STEPS = 2
MESH = pl.DeviceIdType.MESH
F32 = jnp.float32
BF16 = jnp.bfloat16
NN = (((1,), (0,)), ((), ()))
NT = (((1,), (1,)), ((), ()))

courant = 0.3
tumble = 0.2


def mm(a, b, dims=NN):
    return lax.dot_general(a, b, dims, precision=lax.Precision.HIGHEST, preferred_element_type=F32)


def bdot(a, b, dims=NN):
    return lax.dot_general(a, b, dims, preferred_element_type=F32)


def split(a):
    hi = a.astype(BF16)
    return hi, (a - hi.astype(F32)).astype(BF16)


def left3(a):
    hi, lo = split(a)
    return jnp.concatenate([hi, hi, lo], axis=1)


def right3(b):
    hi, lo = split(b)
    return jnp.concatenate([hi, lo, hi], axis=0)


def gram3(left_hi, left_lo, right_hi, right_lo):
    width = right_hi.shape[0]
    first = bdot(left_hi, jnp.concatenate([right_hi, right_lo], axis=0), NT)
    return first[:, :width] + first[:, width:] + bdot(left_lo, right_hi, NT)


def speed_of(density):
    return 1.0 / (1.0 + density * density)


def eliminate(gram):
    n = gram.shape[0]
    rows = lax.broadcasted_iota(jnp.int32, (8, 2 * n), 0)
    lanes = lax.broadcasted_iota(jnp.int32, (n, n), 1)
    eye = jnp.where(lax.broadcasted_iota(jnp.int32, (n, n), 0) == lanes, 1.0, 0.0)
    both = jnp.concatenate([gram, eye], axis=1)
    blocks = [both[8 * b : 8 * b + 8] for b in range(n // 8)]
    for k in range(n):
        kb, ks = divmod(k, 8)
        pivot = blocks[kb][ks : ks + 1, k : k + 1]
        inverse = 1.0 / pivot
        row = blocks[kb][ks : ks + 1, :]
        scaled = row * inverse
        for b in range(kb, n // 8):
            factor = blocks[b][:, k : k + 1]
            update = blocks[b] - factor * scaled
            if b == kb:
                blocks[b] = jnp.where(rows > ks, update, blocks[b])
            else:
                blocks[b] = update
    whole = jnp.concatenate(blocks, axis=0)
    diagonal = jnp.sum(whole[:, :n] * eye, axis=1, keepdims=True)
    whole = whole / jnp.sqrt(diagonal)
    upper = jnp.where(lanes >= lax.broadcasted_iota(jnp.int32, (n, n), 0), whole[:, :n], 0.0)
    return upper, whole[:, n:]


def kernel(
    sizes, x_ref, s_ref, v_ref, d_ref, x_out, s_out, v_out,
    k_s, base_s, tpx_s, tmx_s, t_s, k1_s, h_s, khx_s, khy_s, hhy_s, v_s, yface_s,
    xhalo_s, yhalo_s, pay_s, r1_s, c_s, r2_s, f_s, r3_s,
    hsend, hrecv, asend, arecv,
):
    ngx, ngy, slabs, ylen, zlen = sizes
    slab = ylen * zlen
    nloc = slabs * slab
    chunks = slab // 128
    cells = float(nloc * ngx * ngy)
    no = v_ref.shape[0]
    rank = 64
    c, t = courant, tumble
    me_x, me_y = lax.axis_index("gx"), lax.axis_index("gy")
    crow = 256 // ngy

    barrier = pltpu.get_barrier_semaphore()

    def greet_x(i, _):
        pl.semaphore_signal(barrier, inc=1, device_id={"gx": lax.rem(me_x + i, ngx), "gy": me_y}, device_id_type=MESH)
        return 0

    def greet_y(i, _):
        pl.semaphore_signal(barrier, inc=1, device_id={"gx": me_x, "gy": lax.rem(me_y + i, ngy)}, device_id_type=MESH)
        return 0

    lax.fori_loop(1, ngx, greet_x, 0)
    lax.fori_loop(1, ngy, greet_y, 0)

    eye = jnp.where(
        lax.broadcasted_iota(jnp.int32, (rank, rank), 0) == lax.broadcasted_iota(jnp.int32, (rank, rank), 1), 1.0, 0.0
    )
    lane = lax.broadcasted_iota(jnp.int32, (rank, 128), 1)
    zpos = lax.rem(lane, zlen)
    group = lane // zlen
    per = 128 // zlen

    def cut(a):
        return [a[:, 128 * i : 128 * i + 128] for i in range(a.shape[1] // 128)]

    def roll(a, s):
        s = s % 128
        return a if s == 0 else pltpu.roll(a, s, 1)

    def from_y_before(a, halo, q):
        rolled = [roll(piece, zlen) for piece in cut(a)]
        last = roll(halo, zlen * (-q))
        out = []
        for piece in rolled:
            out.append(jnp.where(lane < zlen, last, piece))
            last = piece
        return jnp.concatenate(out, axis=1)

    def from_y_after(a, halo, q):
        rolled = [roll(piece, -zlen) for piece in cut(a)] + [roll(halo, 128 - zlen - zlen * q)]
        return jnp.concatenate(
            [jnp.where(lane < 128 - zlen, rolled[i], rolled[i + 1]) for i in range(len(rolled) - 1)], axis=1
        )

    def from_z_before(a):
        return jnp.concatenate([jnp.where(zpos == 0, roll(p, 1 - zlen), roll(p, 1)) for p in cut(a)], axis=1)

    def from_z_after(a):
        return jnp.concatenate([jnp.where(zpos == zlen - 1, roll(p, zlen - 1), roll(p, -1)) for p in cut(a)], axis=1)

    def faces(ref):
        first, last = jnp.zeros((rank, 128), F32), jnp.zeros((rank, 128), F32)
        for q in range(slabs):
            low = ref[:, slab * q : slab * q + 128]
            high = ref[:, slab * q + slab - 128 : slab * q + slab]
            first = jnp.where(group == q, roll(low, zlen * q), first)
            last = jnp.where(group == q, roll(high, zlen * q - (128 - zlen)), last)
        return first, last

    def halo_copies(ref, e):
        left = {"gx": lax.rem(me_x + ngx - 1, ngx), "gy": me_y}
        right = {"gx": lax.rem(me_x + 1, ngx), "gy": me_y}
        below = {"gx": me_x, "gy": lax.rem(me_y + ngy - 1, ngy)}
        above = {"gx": me_x, "gy": lax.rem(me_y + 1, ngy)}
        plan = [
            (ref.at[:, pl.ds(nloc - slab, slab)], xhalo_s.at[e, 0], right),
            (ref.at[:, pl.ds(0, slab)], xhalo_s.at[e, 1], left),
            (yface_s.at[e, 1], yhalo_s.at[e, 0], above),
            (yface_s.at[e, 0], yhalo_s.at[e, 1], below),
        ]
        return [
            pltpu.make_async_remote_copy(
                src_ref=src, dst_ref=dst, send_sem=hsend.at[e, i], recv_sem=hrecv.at[e, i], device_id=to, device_id_type=MESH
            )
            for i, (src, dst, to) in enumerate(plan)
        ]

    def spread(phase, step, src_of, dst, mine, n, axis):
        def copy(i):
            to = lax.rem(mine + i, n)
            ids = {"gx": to, "gy": me_y} if axis == "gx" else {"gx": me_x, "gy": to}
            return pltpu.make_async_remote_copy(
                src_ref=src_of(to), dst_ref=dst.at[step, mine], send_sem=asend.at[step, phase, i],
                recv_sem=arecv.at[step, phase, mine], device_id=ids, device_id_type=MESH,
            )

        def start(i, _):
            copy(i).start()
            return 0

        lax.fori_loop(1, n, start, 0)

    def settle(phase, step, src_of, dst, mine, n, axis):
        def wait(i, _):
            source = lax.rem(mine + i, n)
            ids = {"gx": source, "gy": me_y} if axis == "gx" else {"gx": me_x, "gy": source}
            arrived = pltpu.make_async_remote_copy(
                src_ref=src_of(source), dst_ref=dst.at[step, source], send_sem=asend.at[step, phase, i],
                recv_sem=arecv.at[step, phase, source], device_id=ids, device_id_type=MESH,
            )
            arrived.wait_recv()
            arrived.wait_send()
            return 0

        lax.fori_loop(1, n, wait, 0)

    st = left3(mm(eye, s_ref[...], NT))
    for q in range(slabs):
        x_hi, x_lo = split(x_ref[slab * q : slab * q + slab, :])
        k_s[:, slab * q : slab * q + slab] = (
            bdot(st[:, :rank], x_hi, NT) + bdot(st[:, rank : 2 * rank], x_lo, NT) + bdot(st[:, 2 * rank :], x_hi, NT)
        )
    first, last = faces(k_s)
    yface_s[0, 0] = first
    yface_s[0, 1] = last
    pl.semaphore_wait(barrier, ngx + ngy - 2)
    first_halo = halo_copies(k_s, 0)
    for copy in first_halo:
        copy.start()
    for i in range(no // 512):
        v_s[:, 512 * i : 512 * i + 512] = mm(eye, v_ref[512 * i : 512 * i + 512, :], NT)

    def step_body(step):
        total = jnp.zeros((6 * rank + 16, rank), F32)
        for i in range(no // 512):
            v = v_s[:, 512 * i : 512 * i + 512]
            v_hi, v_lo = split(v)
            d = d_ref[:, 512 * i : 512 * i + 512]
            parts = []
            for dim in range(3):
                parts.append(v * jnp.maximum(d[dim : dim + 1], 0.0))
            for dim in range(3):
                parts.append(v * jnp.maximum(-d[dim : dim + 1], 0.0))
            parts.append(jnp.ones((16, 512), F32))
            l_hi, l_lo = split(jnp.concatenate(parts, axis=0))
            total = total + gram3(l_hi, l_lo, v_hi, v_lo)
        total = total * (1.0 / no)
        tables = [total[rank * i : rank * i + rank] for i in range(6)]
        u_row = total[6 * rank : 6 * rank + 1]
        u_col = jnp.sum(eye * u_row, axis=1, keepdims=True)
        center = tables[0] + tables[1] + tables[2] + tables[3] + tables[4] + tables[5]
        stencil = left3(c * jnp.concatenate([center] + tables, axis=0))

        if step == 0:
            for copy in first_halo:
                copy.wait()
            for i in range(2):
                khx_s[i] = xhalo_s[0, i]
                khy_s[i] = yhalo_s[0, i]

        def flux(k):
            density = jnp.sum(k * u_col, axis=0, keepdims=True)
            return density, speed_of(density) * k

        for q in range(slabs):
            k = k_s[:, slab * q : slab * q + slab]
            density, g = flux(k)
            out = bdot(stencil, right3(g))
            base_s[:, slab * q : slab * q + slab] = (1.0 - t) * k + t * u_col * density - out[:rank]
            tpx_s[:, slab * (q + 1) : slab * (q + 2)] = out[rank : 2 * rank]
            tmx_s[:, slab * q : slab * (q + 1)] = out[4 * rank : 5 * rank]
            t_s[0, :, slab * q : slab * q + slab] = out[2 * rank : 3 * rank]
            t_s[1, :, slab * q : slab * q + slab] = out[5 * rank : 6 * rank]
            t_s[2, :, slab * q : slab * q + slab] = out[3 * rank : 4 * rank]
            t_s[3, :, slab * q : slab * q + slab] = out[6 * rank : 7 * rank]
        tpx_s[:, :slab] = bdot(stencil[rank : 2 * rank], right3(flux(khx_s[0])[1]))
        tmx_s[:, slab * slabs :] = bdot(stencil[4 * rank : 5 * rank], right3(flux(khx_s[1])[1]))
        tpy = bdot(stencil[2 * rank : 3 * rank], right3(flux(khy_s[0])[1]))
        tmy = bdot(stencil[5 * rank : 6 * rank], right3(flux(khy_s[1])[1]))
        for q in range(slabs):
            here = slice(slab * q, slab * q + slab)
            k1_s[:, here] = (
                base_s[:, here]
                + tpx_s[:, here]
                + tmx_s[:, slab * (q + 1) : slab * (q + 2)]
                + from_y_before(t_s[0, :, here], tpy, q)
                + from_y_after(t_s[1, :, here], tmy, q)
                + from_z_before(t_s[2, :, here])
                + from_z_after(t_s[3, :, here])
            )
        first, last = faces(k1_s)
        yface_s[step + 1, 0] = first
        yface_s[step + 1, 1] = last
        halo = halo_copies(k1_s, step + 1)
        for copy in halo:
            copy.start()

        for q in range(slabs):
            h_s[:, slab * (q + 1) : slab * (q + 2)] = flux(k1_s[:, slab * q : slab * q + slab])[1]
        for copy in halo:
            copy.wait()
        h_s[:, :slab] = flux(xhalo_s[step + 1, 0])[1]
        h_s[:, slab * (slabs + 1) :] = flux(xhalo_s[step + 1, 1])[1]
        hy = [flux(yhalo_s[step + 1, i])[1] for i in range(2)]
        raw = jnp.zeros((7 * rank, rank), F32)
        for q in range(slabs):
            k1 = k1_s[:, slab * q : slab * q + slab]
            h = h_s[:, slab * (q + 1) : slab * (q + 2)]
            stack = jnp.concatenate(
                [
                    k1,
                    h - h_s[:, slab * q : slab * (q + 1)],
                    h - from_y_before(h, hy[0], q),
                    h - from_z_before(h),
                    h_s[:, slab * (q + 2) : slab * (q + 3)] - h,
                    from_y_after(h, hy[1], q) - h,
                    from_z_after(h) - h,
                ],
                axis=0,
            )
            l_hi, l_lo = split(stack)
            raw = raw + gram3(l_hi, l_lo, l_hi[:rank], l_lo[:rank])
        packed = jnp.concatenate(
            [raw[: 4 * rank], jnp.concatenate([raw[4 * rank :], jnp.zeros((rank, rank), F32)], axis=0)], axis=1
        )
        pay_s[step] = packed.reshape(ngy, crow, 128)

        chunk = lambda j: pay_s.at[step, j]
        spread(0, step, chunk, r1_s, me_y, ngy, "gy")
        r1_s[step, me_y] = pay_s[step, me_y]
        settle(0, step, chunk, r1_s, me_y, ngy, "gy")
        c_s[step] = jnp.sum(r1_s[step], axis=0)
        own = lambda j: c_s.at[step]
        spread(1, step, own, r2_s, me_x, ngx, "gx")
        r2_s[step, me_x] = c_s[step]
        settle(1, step, own, r2_s, me_x, ngx, "gx")
        f_s[step] = jnp.sum(r2_s[step], axis=0)
        summed = lambda j: f_s.at[step]
        spread(2, step, summed, r3_s, me_y, ngy, "gy")
        r3_s[step, me_y] = f_s[step]
        settle(2, step, summed, r3_s, me_y, ngy, "gy")
        full = r3_s[step].reshape(256, 128) * (1.0 / cells)

        upper, inverse = eliminate(full[:rank, :rank])
        z_stack = jnp.concatenate([full[rank:, :rank], full[: 3 * rank, rank:]], axis=0)
        q_wide = mm(inverse, z_stack, NT)
        q_stack = jnp.concatenate([q_wide[:, rank * i : rank * i + rank] for i in range(6)], axis=0)
        m_stack = mm(q_stack, inverse, NT)
        ms = mm(m_stack, upper)
        su = jnp.sum(upper * u_row, axis=1, keepdims=True)
        s2 = (1.0 + t) * upper - t * (su * u_row)
        for dim in range(3):
            s2 = s2 + c * mm(ms[rank * dim : rank * dim + rank], tables[dim])
            s2 = s2 - c * mm(ms[rank * (dim + 3) : rank * (dim + 4)], tables[dim + 3])
        mean = jnp.sum(s2 * u_row, axis=1, keepdims=True)
        left = left3(jnp.concatenate([s2, c * mm(m_stack, s2)], axis=0))
        gram = jnp.zeros((rank, rank), F32)
        for i in range(no // 512):
            here = slice(512 * i, 512 * i + 512)
            out = bdot(left, right3(v_s[:, here]))
            d = d_ref[:, here]
            l1 = (1.0 - t) * out[:rank] + t * mean
            for dim in range(3):
                l1 = l1 - jnp.maximum(d[dim : dim + 1], 0.0) * out[rank * (dim + 1) : rank * (dim + 2)]
                l1 = l1 + jnp.maximum(-d[dim : dim + 1], 0.0) * out[rank * (dim + 4) : rank * (dim + 5)]
            v_s[:, here] = l1
            hi, lo = split(l1)
            gram = gram + gram3(hi, lo, hi, lo)
        v_upper, v_inverse = eliminate(gram * (1.0 / no))
        vi = left3(v_inverse)
        last_step = step == STEPS - 1
        for i in range(no // 512):
            here = slice(512 * i, 512 * i + 512)
            v = bdot(vi, right3(v_s[:, here]))
            if last_step:
                v_out[here, :] = jnp.concatenate([v, v], axis=0).T[:, :rank]
            else:
                v_s[:, here] = v
        if last_step:
            s_out[...] = mm(eye, v_upper, NT)
            wt = left3(inverse)
        else:
            wt = left3(mm(v_upper, inverse))
        for q in range(slabs):
            here = slice(slab * q, slab * q + slab)
            k = bdot(wt, right3(k1_s[:, here]))
            if last_step:
                x_out[here, :] = jnp.concatenate([k, k], axis=0).T[:, :rank]
            else:
                k_s[:, here] = k
        if not last_step:
            for i in range(2):
                khx_s[i] = bdot(wt, right3(xhalo_s[step + 1, i]))
                khy_s[i] = bdot(wt, right3(yhalo_s[step + 1, i]))

    for step in range(STEPS):
        step_body(step)


def solution(mesh):
    ngx, ngy = mesh.shape["gx"], mesh.shape["gy"]

    def shards(spatial, coupling, orient, directions):
        slabs, ylen, zlen, rank = spatial.shape
        slab = ylen * zlen
        nloc = slabs * slab
        no = orient.shape[0]
        crow = 256 // ngy
        vmem = pl.BlockSpec(memory_space=pltpu.VMEM)
        scratch = [
            (rank, nloc), (rank, nloc), (rank, nloc + slab), (rank, nloc + slab), (4, rank, nloc), (rank, nloc),
            (rank, nloc + 2 * slab), (2, rank, slab), (2, rank, 128), (2, rank, 128), (rank, no),
            (STEPS + 1, 2, rank, 128), (STEPS + 1, 2, rank, slab), (STEPS + 1, 2, rank, 128),
            (STEPS, ngy, crow, 128), (STEPS, ngy, crow, 128), (STEPS, crow, 128), (STEPS, ngx, crow, 128),
            (STEPS, crow, 128), (STEPS, ngy, crow, 128),
        ]
        n = max(ngx, ngy)
        x, s, v = pl.pallas_call(
            functools.partial(kernel, (ngx, ngy, slabs, ylen, zlen)),
            out_shape=(
                jax.ShapeDtypeStruct((nloc, rank), F32),
                jax.ShapeDtypeStruct((rank, rank), F32),
                jax.ShapeDtypeStruct((no, rank), F32),
            ),
            in_specs=[vmem] * 4,
            out_specs=(vmem, vmem, vmem),
            scratch_shapes=[pltpu.VMEM(shape, F32) for shape in scratch]
            + [
                pltpu.SemaphoreType.DMA((STEPS + 1, 4)),
                pltpu.SemaphoreType.DMA((STEPS + 1, 4)),
                pltpu.SemaphoreType.DMA((STEPS, 3, n)),
                pltpu.SemaphoreType.DMA((STEPS, 3, n)),
            ],
            compiler_params=pltpu.CompilerParams(
                collective_id=0, has_side_effects=True, vmem_limit_bytes=60 * 1024 * 1024
            ),
        )(spatial.reshape(nloc, rank), coupling, orient, directions)
        return x.reshape(spatial.shape), s, v

    return jax.shard_map(
        shards,
        mesh=mesh,
        in_specs=(P("gx", "gy", None, None), P(), P(), P()),
        out_specs=(P("gx", "gy", None, None), P(), P()),
        check_vma=False,
    )
```

```python
import functools

import jax
import jax.numpy as jnp
from jax import lax
from jax.experimental import pallas as pl
from jax.experimental.pallas import tpu as pltpu
from jax.sharding import PartitionSpec as P

STEPS = 2
MESH = pl.DeviceIdType.MESH
F32 = jnp.float32
BF16 = jnp.bfloat16
NN = (((1,), (0,)), ((), ()))
NT = (((1,), (1,)), ((), ()))

courant = 0.3
tumble = 0.2


def mm(a, b, dims=NN):
    return lax.dot_general(a, b, dims, precision=lax.Precision.HIGHEST, preferred_element_type=F32)


def bdot(a, b, dims=NN):
    return lax.dot_general(a, b, dims, preferred_element_type=F32)


def split(a):
    hi = a.astype(BF16)
    return hi, (a - hi.astype(F32)).astype(BF16)


def left3(a):
    hi, lo = split(a)
    return jnp.concatenate([hi, hi, lo], axis=1)


def right3(b):
    hi, lo = split(b)
    return jnp.concatenate([hi, lo, hi], axis=0)


def gram3(left_hi, left_lo, right_hi, right_lo):
    width = right_hi.shape[0]
    first = bdot(left_hi, jnp.concatenate([right_hi, right_lo], axis=0), NT)
    return first[:, :width] + first[:, width:] + bdot(left_lo, right_hi, NT)


def speed_of(density):
    return 1.0 / (1.0 + density * density)


def begin(gram):
    n = gram.shape[0]
    eye = jnp.where(lax.broadcasted_iota(jnp.int32, (n, n), 0) == lax.broadcasted_iota(jnp.int32, (n, n), 1), 1.0, 0.0)
    both = jnp.concatenate([gram, eye], axis=1)
    return [both[8 * b : 8 * b + 8] for b in range(n // 8)]


def advance(blocks, start, stop):
    width = blocks[0].shape[1]
    below = lax.broadcasted_iota(jnp.int32, (8, width), 0)

    def across(a, c):
        return jnp.broadcast_to(a[:, c : c + 1], (8, width))

    def down(a, r):
        return jnp.broadcast_to(a[r : r + 1], (8, width))

    for kb in range(start, stop):
        own = [across(blocks[kb], 8 * kb + c) for c in range(8)]
        rows, inverses, heads = [], [], []
        current = blocks[kb]
        for k in range(8):
            head = {j: down(own[j], k) for j in range(k, 8)}
            inverse = 1.0 / head[k]
            row = down(current, k)
            factor = jnp.where(below > k, own[k] * inverse, 0.0)
            for j in range(k + 1, 8):
                own[j] = own[j] - factor * head[j]
            current = current - factor * row
            rows.append(row)
            inverses.append(inverse)
            heads.append(head)
        blocks[kb] = current
        for b in range(kb + 1, len(blocks)):
            columns = [across(blocks[b], 8 * kb + c) for c in range(8)]
            for k in range(8):
                factor = columns[k] * inverses[k]
                for j in range(k + 1, 8):
                    columns[j] = columns[j] - factor * heads[k][j]
                blocks[b] = blocks[b] - factor * rows[k]
    return blocks


def finish(blocks):
    whole = jnp.concatenate(blocks, axis=0)
    n = whole.shape[0]
    i, j = (lax.broadcasted_iota(jnp.int32, (n, n), d) for d in range(2))
    diagonal = jnp.sum(jnp.where(i == j, whole[:, :n], 0.0), axis=1, keepdims=True)
    whole = whole * (1.0 / jnp.sqrt(diagonal))
    return jnp.where(j >= i, whole[:, :n], 0.0), whole[:, n:]


def kernel(
    sizes, x_ref, s_ref, v_ref, d_ref, x_out, s_out, v_out,
    k_s, base_s, tpx_s, tmx_s, t_s, k1_s, h_s, khx_s, khy_s, v_s, yface_s,
    xhalo_s, yhalo_s, pay_s, r1_s, c_s, r2_s, f_s, r3_s, den_s, g3_s, kk_s,
    hsend, hrecv, asend, arecv,
):
    ngx, ngy, slabs, ylen, zlen = sizes
    slab = ylen * zlen
    nloc = slabs * slab
    cells = float(nloc * ngx * ngy)
    no = v_ref.shape[1]
    rank = 64
    c, t = courant, tumble
    me_x, me_y = lax.axis_index("gx"), lax.axis_index("gy")
    crow = 128 // ngy
    signs = ((0, 1), (1, 1), (0, -1), (1, -1), (2, 1), (2, -1))

    barrier = pltpu.get_barrier_semaphore()

    def greet_x(i, _):
        pl.semaphore_signal(barrier, inc=1, device_id={"gx": lax.rem(me_x + i, ngx), "gy": me_y}, device_id_type=MESH)
        return 0

    def greet_y(i, _):
        pl.semaphore_signal(barrier, inc=1, device_id={"gx": me_x, "gy": lax.rem(me_y + i, ngy)}, device_id_type=MESH)
        return 0

    lax.fori_loop(1, ngx, greet_x, 0)
    lax.fori_loop(1, ngy, greet_y, 0)

    eye = jnp.where(
        lax.broadcasted_iota(jnp.int32, (rank, rank), 0) == lax.broadcasted_iota(jnp.int32, (rank, rank), 1), 1.0, 0.0
    )
    lane = lax.broadcasted_iota(jnp.int32, (rank, 128), 1)
    zpos = lax.rem(lane, zlen)
    group = lane // zlen

    def at(q):
        return slice(slab * q, slab * q + slab)

    def block(i):
        return slice(rank * i, rank * i + rank)

    def cut(a):
        return [a[:, 128 * i : 128 * i + 128] for i in range(a.shape[1] // 128)]

    def roll(a, s):
        s = s % 128
        return a if s == 0 else pltpu.roll(a, s, 1)

    def from_y_before(a, halo, q):
        last = roll(halo, zlen * (-q))
        out = []
        for piece in [roll(piece, zlen) for piece in cut(a)]:
            out.append(jnp.where(lane < zlen, last, piece))
            last = piece
        return jnp.concatenate(out, axis=1)

    def from_y_after(a, halo, q):
        rolled = [roll(piece, -zlen) for piece in cut(a)] + [roll(halo, 128 - zlen - zlen * q)]
        return jnp.concatenate(
            [jnp.where(lane < 128 - zlen, rolled[i], rolled[i + 1]) for i in range(len(rolled) - 1)], axis=1
        )

    def from_z_before(a):
        return jnp.concatenate([jnp.where(zpos == 0, roll(p, 1 - zlen), roll(p, 1)) for p in cut(a)], axis=1)

    def from_z_after(a):
        return jnp.concatenate([jnp.where(zpos == zlen - 1, roll(p, zlen - 1), roll(p, -1)) for p in cut(a)], axis=1)

    def faces(ref, e):
        first, last = jnp.zeros((rank, 128), F32), jnp.zeros((rank, 128), F32)
        for q in range(slabs):
            low = ref[:, slab * q : slab * q + 128]
            high = ref[:, slab * q + slab - 128 : slab * q + slab]
            first = jnp.where(group == q, roll(low, zlen * q), first)
            last = jnp.where(group == q, roll(high, zlen * q - (128 - zlen)), last)
        yface_s[e, 0] = first
        yface_s[e, 1] = last

    def halo_copies(ref, e):
        left = {"gx": lax.rem(me_x + ngx - 1, ngx), "gy": me_y}
        right = {"gx": lax.rem(me_x + 1, ngx), "gy": me_y}
        under = {"gx": me_x, "gy": lax.rem(me_y + ngy - 1, ngy)}
        over = {"gx": me_x, "gy": lax.rem(me_y + 1, ngy)}
        plan = [
            (ref.at[:, pl.ds(0, slab)], xhalo_s.at[e, 1], left),
            (ref.at[:, pl.ds(nloc - slab, slab)], xhalo_s.at[e, 0], right),
            (yface_s.at[e, 1], yhalo_s.at[e, 0], over),
            (yface_s.at[e, 0], yhalo_s.at[e, 1], under),
        ]
        return [
            pltpu.make_async_remote_copy(
                src_ref=src, dst_ref=dst, send_sem=hsend.at[e, i], recv_sem=hrecv.at[e, i], device_id=to, device_id_type=MESH
            )
            for i, (src, dst, to) in enumerate(plan)
        ]

    def phase_copy(a, phase, i, arriving):
        mine, n = (me_x, ngx) if phase == 1 else (me_y, ngy)
        other = lax.rem(mine + i, n)
        ids = {"gx": other, "gy": me_y} if phase == 1 else {"gx": me_x, "gy": other}
        src = pay_s.at[a, other] if phase == 0 else (c_s if phase == 1 else f_s).at[a]
        slot = other if arriving else mine
        return pltpu.make_async_remote_copy(
            src_ref=src, dst_ref=(r1_s, r2_s, r3_s)[phase].at[a, slot], send_sem=asend.at[a, phase, i],
            recv_sem=arecv.at[a, phase, slot], device_id=ids, device_id_type=MESH,
        )

    def start_phase(a, phase):
        def one(i, _):
            phase_copy(a, phase, i, False).start()
            return 0

        lax.fori_loop(1, ngx if phase == 1 else ngy, one, 0)
        if phase == 0:
            r1_s[a, me_y] = pay_s[a, me_y]
        elif phase == 1:
            r2_s[a, me_x] = c_s[a]
        else:
            r3_s[a, me_y] = f_s[a]

    def end_phase(a, phase):
        def one(i, _):
            copy = phase_copy(a, phase, i, True)
            copy.wait_recv()
            copy.wait_send()
            return 0

        lax.fori_loop(1, ngx if phase == 1 else ngy, one, 0)
        if phase == 0:
            c_s[a] = jnp.sum(r1_s[a], axis=0)
        elif phase == 1:
            f_s[a] = jnp.sum(r2_s[a], axis=0)

    def pack(a, raw):
        pay_s[a] = jnp.concatenate([raw[: 2 * rank], raw[2 * rank :]], axis=1).reshape(ngy, crow, 128)

    def unpack(a):
        full = r3_s[a].reshape(128, 128) * (1.0 / cells)
        return jnp.concatenate([full[:, :rank], full[:, rank:]], axis=0)

    def tables_of(ref):
        total = jnp.zeros((6 * rank + 16, rank), F32)
        for i in range(no // 512):
            v = ref[:, 512 * i : 512 * i + 512]
            v_hi, v_lo = split(v)
            d = d_ref[:, 512 * i : 512 * i + 512]
            parts = [v * jnp.maximum(sign * d[dim : dim + 1], 0.0) for dim, sign in signs]
            l_hi, l_lo = split(jnp.concatenate(parts + [jnp.ones((16, 512), F32)], axis=0))
            total = total + gram3(l_hi, l_lo, v_hi, v_lo)
        total = total * (1.0 / no)
        return total[: 6 * rank], total[6 * rank : 6 * rank + 1]

    def column(row):
        return jnp.sum(eye * row, axis=1, keepdims=True)

    def flux(k, u_col):
        density = jnp.sum(k * u_col, axis=0, keepdims=True)
        return density, speed_of(density) * k

    def prepare(u_col):
        for q in range(slabs):
            density, g = flux(k_s[:, at(q)], u_col)
            den_s[:, at(q)] = density
            g3_s[:, at(q)] = right3(g)

    def prepare_halo(u_col):
        for i in range(2):
            g3_s[:, nloc + slab * i : nloc + slab * (i + 1)] = right3(flux(khx_s[i], u_col)[1])
            at_y = nloc + 2 * slab + 128 * i
            g3_s[:, at_y : at_y + 128] = right3(flux(khy_s[i], u_col)[1])

    st = left3(mm(eye, s_ref[...], NT))
    first_halo = halo_copies(k_s, 0)
    for q in (0, slabs - 1) + tuple(range(1, slabs - 1)):
        x_hi, x_lo = split(x_ref[at(q), :])
        k_s[:, at(q)] = bdot(st[:, :rank], x_hi, NT) + bdot(st[:, rank : 2 * rank], x_lo, NT) + bdot(st[:, 2 * rank :], x_hi, NT)
    faces(k_s, 0)
    pl.semaphore_wait(barrier, ngx + ngy - 2)
    for copy in first_halo:
        copy.start()
    tables, u_row = tables_of(v_ref)
    u_col = column(u_row)
    weights = tables
    prepare(u_col)
    for copy in first_halo:
        copy.wait()
    for i in range(2):
        khx_s[i] = xhalo_s[0, i]
        khy_s[i] = yhalo_s[0, i]
    prepare_halo(u_col)
    k_left = None
    v_now = v_ref

    for step in range(STEPS):
        last_step = step == STEPS - 1
        center = weights[block(0)] + weights[block(1)] + weights[block(2)]
        center = center + weights[block(3)] + weights[block(4)] + weights[block(5)]
        stencil = left3(c * jnp.concatenate([center, weights], axis=0))
        bx = nloc
        by = nloc + 2 * slab
        tpx_s[:, :slab] = bdot(stencil[block(1)], g3_s[:, bx : bx + slab])
        tmx_s[:, slab * slabs :] = bdot(stencil[block(3)], g3_s[:, bx + slab : bx + 2 * slab])
        tpy = bdot(stencil[block(2)], g3_s[:, by : by + 128])
        tmy = bdot(stencil[block(4)], g3_s[:, by + 128 : by + 256])
        for q in range(slabs):
            k = k_s[:, at(q)]
            if k_left is not None:
                k = bdot(k_left, right3(k))
            out = bdot(stencil, g3_s[:, at(q)])
            base_s[:, at(q)] = (1.0 - t) * k + t * u_col * den_s[:, at(q)] - out[:rank]
            tpx_s[:, at(q + 1)] = out[block(1)]
            t_s[0, :, at(q)] = out[block(2)]
            tmx_s[:, at(q)] = out[block(3)]
            t_s[1, :, at(q)] = out[block(4)]
            t_s[2, :, at(q)] = out[block(5)]
            t_s[3, :, at(q)] = out[block(6)]
        halo = halo_copies(k1_s, step + 1)
        for q in (0, slabs - 1) + tuple(range(1, slabs - 1)):
            k1_s[:, at(q)] = (
                base_s[:, at(q)]
                + tpx_s[:, at(q)]
                + tmx_s[:, at(q + 1)]
                + from_y_before(t_s[0, :, at(q)], tpy, q)
                + from_y_after(t_s[1, :, at(q)], tmy, q)
                + from_z_before(t_s[2, :, at(q)])
                + from_z_after(t_s[3, :, at(q)])
            )
            if q == 0:
                halo[0].start()
            elif q == slabs - 1:
                halo[1].start()
        faces(k1_s, step + 1)
        halo[2].start()
        halo[3].start()

        first, second = 2 * step, 2 * step + 1
        raw = jnp.zeros((3 * rank, rank), F32)
        for q in range(slabs):
            k1 = k1_s[:, at(q)]
            h = flux(k1, u_col)[1]
            h_s[:, at(q + 1)] = h
            l_hi, l_lo = split(jnp.concatenate([k1, h - from_z_before(h), from_z_after(h) - h], axis=0))
            kk_s[:rank, at(q)] = l_hi[:rank]
            kk_s[rank:, at(q)] = l_lo[:rank]
            raw = raw + gram3(l_hi, l_lo, l_hi[:rank], l_lo[:rank])
        pack(first, jnp.concatenate([raw, jnp.zeros((rank, rank), F32)], axis=0))
        start_phase(first, 0)
        for copy in halo:
            copy.wait()
        h_s[:, :slab] = flux(xhalo_s[step + 1, 0], u_col)[1]
        h_s[:, slab * (slabs + 1) :] = flux(xhalo_s[step + 1, 1], u_col)[1]
        hy = [flux(yhalo_s[step + 1, i], u_col)[1] for i in range(2)]
        raw = jnp.zeros((4 * rank, rank), F32)
        for q in range(slabs):
            h = h_s[:, at(q + 1)]
            l_hi, l_lo = split(
                jnp.concatenate(
                    [
                        h - h_s[:, at(q)],
                        h - from_y_before(h, hy[0], q),
                        h_s[:, at(q + 2)] - h,
                        from_y_after(h, hy[1], q) - h,
                    ],
                    axis=0,
                )
            )
            raw = raw + gram3(l_hi, l_lo, kk_s[:rank, at(q)], kk_s[rank:, at(q)])
        pack(second, raw)
        start_phase(second, 0)
        for phase in range(2):
            for a in (first, second):
                end_phase(a, phase)
                start_phase(a, phase + 1)
        end_phase(first, 2)
        total = unpack(first)
        upper, inverse = finish(advance(begin(total[:rank]), 0, rank // 8))
        inverse_t = mm(eye, inverse, NT)
        q_z = mm(inverse, total[rank : 3 * rank], NT)
        signed = jnp.concatenate([tables[: 2 * rank], -tables[2 * rank : 4 * rank], tables[block(4)], -tables[block(5)]], axis=0)
        s_start = (1.0 + t) * upper - t * (jnp.sum(upper * u_row, axis=1, keepdims=True) * u_row)
        s_start = s_start + c * mm(q_z, signed[4 * rank :])
        left = left3(inverse)
        for q in range(slabs):
            x1 = bdot(left, right3(k1_s[:, at(q)]))
            if last_step:
                x_out[at(q), :] = jnp.concatenate([x1, x1], axis=0).T[:, :rank]
            else:
                k_s[:, at(q)] = x1
        if not last_step:
            for i in range(2):
                khx_s[i] = bdot(left, right3(xhalo_s[step + 1, i]))
                khy_s[i] = bdot(left, right3(yhalo_s[step + 1, i]))
        end_phase(second, 2)
        q_xy = mm(inverse, unpack(second), NT)
        s2 = s_start + c * mm(q_xy, signed[: 4 * rank])
        wide = jnp.concatenate([q_xy, q_z], axis=1)
        q_stack = jnp.concatenate([wide[:, block(i)] for i in range(6)], axis=0)
        ms2 = mm(q_stack, mm(inverse_t, s2))
        mean = jnp.sum(s2 * u_row, axis=1, keepdims=True)
        left = left3(jnp.concatenate([(1.0 - t) * s2, c * ms2], axis=0))
        gram = jnp.zeros((rank, rank), F32)
        for i in range(no // 512):
            here = slice(512 * i, 512 * i + 512)
            out = bdot(left, right3(v_now[:, here]))
            d = d_ref[:, here]
            l1 = out[:rank] + t * mean
            for j, (dim, sign) in enumerate(signs):
                l1 = l1 - (sign * jnp.maximum(sign * d[dim : dim + 1], 0.0)) * out[block(j + 1)]
            v_s[:, here] = l1
            hi, lo = split(l1)
            gram = gram + gram3(hi, lo, hi, lo)
        v_now = v_s
        v_upper, v_inverse = finish(advance(begin(gram * (1.0 / no)), 0, rank // 8))
        if last_step:
            left = left3(v_inverse)
            for i in range(no // 512):
                here = slice(512 * i, 512 * i + 512)
                v_out[:, here] = bdot(left, right3(v_s[:, here]))
            s_out[...] = mm(eye, v_upper, NT)
        else:
            raw_tables, raw_row = tables_of(v_s)
            raw_col = column(raw_row)
            prepare(raw_col)
            prepare_halo(raw_col)
            left = left3(v_inverse)
            wide = mm(v_inverse, raw_tables, NT)
            weights = jnp.concatenate([wide[:, block(i)] for i in range(6)], axis=0)
            tables = mm(weights, v_inverse, NT)
            u_col = jnp.sum(v_inverse * raw_row, axis=1, keepdims=True)
            u_row = jnp.sum(eye * u_col, axis=0, keepdims=True)
            k_left = left3(v_upper)
            for i in range(no // 512):
                here = slice(512 * i, 512 * i + 512)
                v_s[:, here] = bdot(left, right3(v_s[:, here]))


def solution(mesh):
    ngx, ngy = mesh.shape["gx"], mesh.shape["gy"]

    def shards(spatial, coupling, orient, directions):
        slabs, ylen, zlen, rank = spatial.shape
        slab = ylen * zlen
        nloc = slabs * slab
        no = orient.shape[0]
        crow = 128 // ngy
        vmem = pl.BlockSpec(memory_space=pltpu.VMEM)
        sums = 2 * STEPS
        scratch = [
            (rank, nloc), (rank, nloc), (rank, nloc + slab), (rank, nloc + slab), (4, rank, nloc), (rank, nloc),
            (rank, nloc + 2 * slab), (2, rank, slab), (2, rank, 128), (rank, no),
            (STEPS + 1, 2, rank, 128), (STEPS + 1, 2, rank, slab), (STEPS + 1, 2, rank, 128),
            (sums, ngy, crow, 128), (sums, ngy, crow, 128), (sums, crow, 128), (sums, ngx, crow, 128),
            (sums, crow, 128), (sums, ngy, crow, 128), (1, nloc),
        ]
        n = max(ngx, ngy)
        x, s, v = pl.pallas_call(
            functools.partial(kernel, (ngx, ngy, slabs, ylen, zlen)),
            out_shape=(
                jax.ShapeDtypeStruct((nloc, rank), F32),
                jax.ShapeDtypeStruct((rank, rank), F32),
                jax.ShapeDtypeStruct((rank, no), F32),
            ),
            in_specs=[vmem] * 4,
            out_specs=(vmem, vmem, vmem),
            scratch_shapes=[pltpu.VMEM(shape, F32) for shape in scratch]
            + [
                pltpu.VMEM((3 * rank, nloc + 2 * slab + 256), BF16),
                pltpu.VMEM((2 * rank, nloc), BF16),
                pltpu.SemaphoreType.DMA((STEPS + 1, 4)),
                pltpu.SemaphoreType.DMA((STEPS + 1, 4)),
                pltpu.SemaphoreType.DMA((sums, 3, n)),
                pltpu.SemaphoreType.DMA((sums, 3, n)),
            ],
            compiler_params=pltpu.CompilerParams(
                collective_id=0, has_side_effects=True, vmem_limit_bytes=40 * 1024 * 1024
            ),
        )(spatial.reshape(nloc, rank), coupling, orient.T, directions)
        return x.reshape(spatial.shape), s, v.T

    return jax.shard_map(
        shards,
        mesh=mesh,
        in_specs=(P("gx", "gy", None, None), P(), P(), P()),
        out_specs=(P("gx", "gy", None, None), P(), P()),
        check_vma=False,
    )
```

```python
import functools

import jax
import jax.numpy as jnp
from jax import lax
from jax.experimental import pallas as pl
from jax.experimental.pallas import tpu as pltpu
from jax.sharding import PartitionSpec as P

STEPS = 2
MESH = pl.DeviceIdType.MESH
F32 = jnp.float32
BF16 = jnp.bfloat16
NN = (((1,), (0,)), ((), ()))
NT = (((1,), (1,)), ((), ()))

courant = 0.3
tumble = 0.2


def mm(a, b, dims=NN):
    return lax.dot_general(a, b, dims, precision=lax.Precision.HIGHEST, preferred_element_type=F32)


def bdot(a, b, dims=NN):
    return lax.dot_general(a, b, dims, preferred_element_type=F32)


def split(a):
    hi = a.astype(BF16)
    return hi, (a - hi.astype(F32)).astype(BF16)


def left3(a):
    hi, lo = split(a)
    return jnp.concatenate([hi, hi, lo], axis=1)


def right3(b):
    hi, lo = split(b)
    return jnp.concatenate([hi, lo, hi], axis=0)


def gram3(left_hi, left_lo, right_hi, right_lo):
    width = right_hi.shape[0]
    first = bdot(left_hi, jnp.concatenate([right_hi, right_lo], axis=0), NT)
    return first[:, :width] + first[:, width:] + bdot(left_lo, right_hi, NT)


def speed_of(density):
    return 1.0 / (1.0 + density * density)


def begin(gram):
    n = gram.shape[0]
    eye = jnp.where(lax.broadcasted_iota(jnp.int32, (n, n), 0) == lax.broadcasted_iota(jnp.int32, (n, n), 1), 1.0, 0.0)
    both = jnp.concatenate([gram, eye], axis=1)
    return [both[8 * b : 8 * b + 8] for b in range(n // 8)]


def advance(blocks, start, stop):
    width = blocks[0].shape[1]
    below = lax.broadcasted_iota(jnp.int32, (8, width), 0)

    def across(a, c):
        return jnp.broadcast_to(a[:, c : c + 1], (8, width))

    def down(a, r):
        return jnp.broadcast_to(a[r : r + 1], (8, width))

    for kb in range(start, stop):
        own = [across(blocks[kb], 8 * kb + c) for c in range(8)]
        rows, inverses, heads = [], [], []
        current = blocks[kb]
        for k in range(8):
            head = {j: down(own[j], k) for j in range(k, 8)}
            inverse = 1.0 / head[k]
            row = down(current, k)
            factor = jnp.where(below > k, own[k] * inverse, 0.0)
            for j in range(k + 1, 8):
                own[j] = own[j] - factor * head[j]
            current = current - factor * row
            rows.append(row)
            inverses.append(inverse)
            heads.append(head)
        blocks[kb] = current
        for b in range(kb + 1, len(blocks)):
            columns = [across(blocks[b], 8 * kb + c) for c in range(8)]
            for k in range(8):
                factor = columns[k] * inverses[k]
                for j in range(k + 1, 8):
                    columns[j] = columns[j] - factor * heads[k][j]
                blocks[b] = blocks[b] - factor * rows[k]
    return blocks


def finish(blocks):
    whole = jnp.concatenate(blocks, axis=0)
    n = whole.shape[0]
    i, j = (lax.broadcasted_iota(jnp.int32, (n, n), d) for d in range(2))
    diagonal = jnp.sum(jnp.where(i == j, whole[:, :n], 0.0), axis=1, keepdims=True)
    whole = whole * (1.0 / jnp.sqrt(diagonal))
    return jnp.where(j >= i, whole[:, :n], 0.0), whole[:, n:]


def kernel(
    sizes, x_hbm, s_hbm, v_hbm, d_hbm, x_out, s_out, v_out, x_ref, s_ref, v_ref, d_ref,
    k_s, base_s, tpx_s, tmx_s, t_s, k1_s, h_s, khx_s, khy_s, v_s, yface_s,
    xhalo_s, yhalo_s, pay_s, r1_s, c_s, r2_s, f_s, r3_s, den_s, g3_s, kk_s, hh_s,
    isem, hsend, hrecv, asend, arecv,
):
    ngx, ngy, slabs, ylen, zlen = sizes
    slab = ylen * zlen
    nloc = slabs * slab
    cells = float(nloc * ngx * ngy)
    no = v_hbm.shape[1]
    rank = 64
    c, t = courant, tumble
    me_x, me_y = lax.axis_index("gx"), lax.axis_index("gy")
    crow = 128 // ngy
    signs = ((0, 1), (1, 1), (0, -1), (1, -1), (2, 1), (2, -1))

    barrier = pltpu.get_barrier_semaphore()

    def greet_x(i, _):
        pl.semaphore_signal(barrier, inc=1, device_id={"gx": lax.rem(me_x + i, ngx), "gy": me_y}, device_id_type=MESH)
        return 0

    def greet_y(i, _):
        pl.semaphore_signal(barrier, inc=1, device_id={"gx": me_x, "gy": lax.rem(me_y + i, ngy)}, device_id_type=MESH)
        return 0

    lax.fori_loop(1, ngx, greet_x, 0)
    lax.fori_loop(1, ngy, greet_y, 0)

    order = (0, slabs - 1) + tuple(range(1, slabs - 1))
    inputs = [pltpu.make_async_copy(s_hbm, s_ref, isem.at[0])]
    for q in order:
        rows = pl.ds(slab * q, slab)
        inputs.append(pltpu.make_async_copy(x_hbm.at[rows], x_ref.at[rows], isem.at[1 + q]))
    inputs.append(pltpu.make_async_copy(v_hbm, v_ref, isem.at[slabs + 1]))
    inputs.append(pltpu.make_async_copy(d_hbm, d_ref, isem.at[slabs + 2]))
    for copy in inputs:
        copy.start()

    eye = jnp.where(
        lax.broadcasted_iota(jnp.int32, (rank, rank), 0) == lax.broadcasted_iota(jnp.int32, (rank, rank), 1), 1.0, 0.0
    )
    lane = lax.broadcasted_iota(jnp.int32, (rank, 128), 1)
    zpos = lax.rem(lane, zlen)
    group = lane // zlen

    def at(q):
        return slice(slab * q, slab * q + slab)

    def block(i):
        return slice(rank * i, rank * i + rank)

    def cut(a):
        return [a[:, 128 * i : 128 * i + 128] for i in range(a.shape[1] // 128)]

    def roll(a, s):
        s = s % 128
        return a if s == 0 else pltpu.roll(a, s, 1)

    def from_y_before(a, halo=None, q=0):
        last = 0.0 if halo is None else roll(halo, zlen * (-q))
        out = []
        for piece in [roll(piece, zlen) for piece in cut(a)]:
            out.append(jnp.where(lane < zlen, last, piece))
            last = piece
        return jnp.concatenate(out, axis=1)

    def from_y_after(a, halo=None, q=0):
        rolled = [roll(piece, -zlen) for piece in cut(a)]
        rolled.append(0.0 if halo is None else roll(halo, 128 - zlen - zlen * q))
        return jnp.concatenate(
            [jnp.where(lane < 128 - zlen, rolled[i], rolled[i + 1]) for i in range(len(rolled) - 1)], axis=1
        )

    def from_z_before(a):
        return jnp.concatenate([jnp.where(zpos == 0, roll(p, 1 - zlen), roll(p, 1)) for p in cut(a)], axis=1)

    def from_z_after(a):
        return jnp.concatenate([jnp.where(zpos == zlen - 1, roll(p, zlen - 1), roll(p, -1)) for p in cut(a)], axis=1)

    def faces(ref, e):
        first, last = jnp.zeros((rank, 128), F32), jnp.zeros((rank, 128), F32)
        for q in range(slabs):
            low = ref[:, slab * q : slab * q + 128]
            high = ref[:, slab * q + slab - 128 : slab * q + slab]
            first = jnp.where(group == q, roll(low, zlen * q), first)
            last = jnp.where(group == q, roll(high, zlen * q - (128 - zlen)), last)
        yface_s[e, 0] = first
        yface_s[e, 1] = last

    def halo_copies(ref, e):
        left = {"gx": lax.rem(me_x + ngx - 1, ngx), "gy": me_y}
        right = {"gx": lax.rem(me_x + 1, ngx), "gy": me_y}
        under = {"gx": me_x, "gy": lax.rem(me_y + ngy - 1, ngy)}
        over = {"gx": me_x, "gy": lax.rem(me_y + 1, ngy)}
        plan = [
            (ref.at[:, pl.ds(0, slab)], xhalo_s.at[e, 1], left),
            (ref.at[:, pl.ds(nloc - slab, slab)], xhalo_s.at[e, 0], right),
            (yface_s.at[e, 1], yhalo_s.at[e, 0], over),
            (yface_s.at[e, 0], yhalo_s.at[e, 1], under),
        ]
        return [
            pltpu.make_async_remote_copy(
                src_ref=src, dst_ref=dst, send_sem=hsend.at[e, i], recv_sem=hrecv.at[e, i], device_id=to, device_id_type=MESH
            )
            for i, (src, dst, to) in enumerate(plan)
        ]

    landing = (r1_s, r2_s, r3_s)

    def start_phase(a, phase):
        mine, n = (me_x, ngx) if phase == 1 else (me_y, ngy)
        for i in sorted(range(1, n), key=lambda i: -min(i, n - i)):
            other = lax.rem(mine + i, n)
            pltpu.make_async_remote_copy(
                src_ref=pay_s.at[a, other] if phase == 0 else (c_s if phase == 1 else f_s).at[a],
                dst_ref=landing[phase].at[a, mine],
                send_sem=asend.at[a, phase],
                recv_sem=arecv.at[a, phase],
                device_id={"gx": other, "gy": me_y} if phase == 1 else {"gx": me_x, "gy": other},
                device_id_type=MESH,
            ).start()
        if phase == 0:
            r1_s[a, me_y] = pay_s[a, me_y]
        elif phase == 1:
            r2_s[a, me_x] = c_s[a]
        else:
            r3_s[a, me_y] = f_s[a]

    def all_of(a, phase, sem):
        part = landing[phase].at[a, pl.ds(0, (ngx if phase == 1 else ngy) - 1)]
        return pltpu.make_async_copy(part, part, sem.at[a, phase])

    def end_phase(a, phase):
        all_of(a, phase, arecv).wait()
        if phase == 0:
            c_s[a] = jnp.sum(r1_s[a], axis=0)
        elif phase == 1:
            f_s[a] = jnp.sum(r2_s[a], axis=0)

    def pack(a, raw):
        pay_s[a] = jnp.concatenate([raw[: 2 * rank], raw[2 * rank :]], axis=1).reshape(ngy, crow, 128)

    def unpack(a):
        full = r3_s[a].reshape(128, 128) * (1.0 / cells)
        return jnp.concatenate([full[:, :rank], full[:, rank:]], axis=0)

    def tables_of(ref):
        total = jnp.zeros((6 * rank + 16, rank), F32)
        for i in range(no // 512):
            v = ref[:, 512 * i : 512 * i + 512]
            v_hi, v_lo = split(v)
            d = d_ref[:, 512 * i : 512 * i + 512]
            parts = [v * jnp.maximum(sign * d[dim : dim + 1], 0.0) for dim, sign in signs]
            l_hi, l_lo = split(jnp.concatenate(parts + [jnp.ones((16, 512), F32)], axis=0))
            total = total + gram3(l_hi, l_lo, v_hi, v_lo)
        total = total * (1.0 / no)
        return total[: 6 * rank], total[6 * rank : 6 * rank + 1]

    def column(row):
        return jnp.sum(eye * row, axis=1, keepdims=True)

    def flux(k, u_col):
        density = jnp.sum(k * u_col, axis=0, keepdims=True)
        return density, speed_of(density) * k

    def prepare(u_col):
        for q in range(slabs):
            density, g = flux(k_s[:, at(q)], u_col)
            den_s[:, at(q)] = density
            g3_s[:, at(q)] = right3(g)

    def prepare_halo(u_col):
        for i in range(2):
            g3_s[:, nloc + slab * i : nloc + slab * (i + 1)] = right3(flux(khx_s[i], u_col)[1])
            at_y = nloc + 2 * slab + 128 * i
            g3_s[:, at_y : at_y + 128] = right3(flux(khy_s[i], u_col)[1])

    inputs[0].wait()
    st = left3(mm(eye, s_ref[...], NT))
    first_halo = halo_copies(k_s, 0)
    for i, q in enumerate(order):
        inputs[1 + i].wait()
        x_hi, x_lo = split(x_ref[at(q), :])
        k_s[:, at(q)] = bdot(st[:, :rank], x_hi, NT) + bdot(st[:, rank : 2 * rank], x_lo, NT) + bdot(st[:, 2 * rank :], x_hi, NT)
    faces(k_s, 0)
    pl.semaphore_wait(barrier, ngx + ngy - 2)
    for copy in first_halo:
        copy.start()
    inputs[slabs + 1].wait()
    inputs[slabs + 2].wait()
    tables, u_row = tables_of(v_ref)
    u_col = column(u_row)
    weights = tables
    prepare(u_col)
    for copy in first_halo:
        copy.wait()
    for i in range(2):
        khx_s[i] = xhalo_s[0, i]
        khy_s[i] = yhalo_s[0, i]
    prepare_halo(u_col)
    k_left = None
    v_now = v_ref
    later = None

    for step in range(STEPS):
        last_step = step == STEPS - 1
        center = weights[block(0)] + weights[block(1)] + weights[block(2)]
        center = center + weights[block(3)] + weights[block(4)] + weights[block(5)]
        stencil = left3(c * jnp.concatenate([center, weights], axis=0))
        bx = nloc
        by = nloc + 2 * slab
        tpx_s[:, :slab] = bdot(stencil[block(1)], g3_s[:, bx : bx + slab])
        tmx_s[:, slab * slabs :] = bdot(stencil[block(3)], g3_s[:, bx + slab : bx + 2 * slab])
        tpy = bdot(stencil[block(2)], g3_s[:, by : by + 128])
        tmy = bdot(stencil[block(4)], g3_s[:, by + 128 : by + 256])
        halo = halo_copies(k1_s, step + 1)

        def spread(q):
            k = k_s[:, at(q)]
            if k_left is not None:
                k = bdot(k_left, right3(k))
            out = bdot(stencil, g3_s[:, at(q)])
            base_s[:, at(q)] = (1.0 - t) * k + t * u_col * den_s[:, at(q)] - out[:rank]
            tpx_s[:, at(q + 1)] = out[block(1)]
            t_s[0, :, at(q)] = out[block(2)]
            tmx_s[:, at(q)] = out[block(3)]
            t_s[1, :, at(q)] = out[block(4)]
            t_s[2, :, at(q)] = out[block(5)]
            t_s[3, :, at(q)] = out[block(6)]

        def combine(q):
            k1_s[:, at(q)] = (
                base_s[:, at(q)]
                + tpx_s[:, at(q)]
                + tmx_s[:, at(q + 1)]
                + from_y_before(t_s[0, :, at(q)], tpy, q)
                + from_y_after(t_s[1, :, at(q)], tmy, q)
                + from_z_before(t_s[2, :, at(q)])
                + from_z_after(t_s[3, :, at(q)])
            )

        spread(0)
        spread(1)
        combine(0)
        halo[0].start()
        for q in range(slabs - 1, 1, -1):
            spread(q)
        combine(slabs - 1)
        halo[1].start()
        for q in range(1, slabs - 1):
            combine(q)
        faces(k1_s, step + 1)
        halo[2].start()
        halo[3].start()

        first, second = 2 * step, 2 * step + 1
        raw = jnp.zeros((4 * rank, rank), F32)
        for q in range(slabs):
            k1 = k1_s[:, at(q)]
            h = flux(k1, u_col)[1]
            h_s[:, at(q)] = h
            l_hi, l_lo = split(jnp.concatenate([k1, h - from_z_before(h), from_z_after(h) - h, h], axis=0))
            kk_s[0, :, at(q)], kk_s[1, :, at(q)] = l_hi[:rank], l_lo[:rank]
            hh_s[0, :, at(q)], hh_s[1, :, at(q)] = l_hi[3 * rank :], l_lo[3 * rank :]
            raw = raw + gram3(l_hi, l_lo, l_hi[:rank], l_lo[:rank])
        pack(first, raw)
        start_phase(first, 0)
        h_k1 = raw[3 * rank :]
        if later is not None:
            tables = later()

        sums = {name: jnp.zeros((rank, rank), F32) for name in ("x-", "y-", "x+", "y+")}
        for q in range(slabs):
            h = h_s[:, at(q)]
            y_hi, y_lo = split(jnp.concatenate([from_y_before(h), from_y_after(h)], axis=0))
            names, his, los = ["y-", "y+"], [y_hi], [y_lo]
            for name, other in (("x-", q - 1), ("x+", q + 1)):
                if 0 <= other < slabs:
                    names.append(name)
                    his.append(hh_s[0, :, at(other)])
                    los.append(hh_s[1, :, at(other)])
            out = gram3(jnp.concatenate(his, axis=0), jnp.concatenate(los, axis=0), kk_s[0, :, at(q)], kk_s[1, :, at(q)])
            for i, name in enumerate(names):
                sums[name] = sums[name] + out[block(i)]
        y_first, y_last = split(yface_s[step + 1, 0]), split(yface_s[step + 1, 1])
        for copy in halo:
            copy.wait()
        for i, (name, edge) in enumerate((("x-", 0), ("x+", slabs - 1))):
            hi, lo = split(flux(xhalo_s[step + 1, i], u_col)[1])
            sums[name] = sums[name] + gram3(hi, lo, kk_s[0, :, at(edge)], kk_s[1, :, at(edge)])
        for i, (name, edge) in enumerate((("y-", y_first), ("y+", y_last))):
            hi, lo = split(flux(yhalo_s[step + 1, i], u_col)[1])
            sums[name] = sums[name] + gram3(hi, lo, *edge)
        pack(
            second,
            jnp.concatenate([h_k1 - sums["x-"], h_k1 - sums["y-"], sums["x+"] - h_k1, sums["y+"] - h_k1], axis=0),
        )
        start_phase(second, 0)
        for phase in range(2):
            for a in (first, second):
                end_phase(a, phase)
                start_phase(a, phase + 1)
        end_phase(first, 2)
        total = unpack(first)
        upper, inverse = finish(advance(begin(total[:rank]), 0, rank // 8))
        inverse_t = mm(eye, inverse, NT)
        q_z = mm(inverse, total[rank : 3 * rank], NT)
        signed = jnp.concatenate([tables[: 2 * rank], -tables[2 * rank : 4 * rank], tables[block(4)], -tables[block(5)]], axis=0)
        s_start = (1.0 + t) * upper - t * (jnp.sum(upper * u_row, axis=1, keepdims=True) * u_row)
        s_start = s_start + c * mm(q_z, signed[4 * rank :])
        left = left3(inverse)
        for q in range(slabs):
            x1 = bdot(left, right3(k1_s[:, at(q)]))
            if last_step:
                x_out[at(q), :] = jnp.concatenate([x1, x1], axis=0).T[:, :rank]
            else:
                k_s[:, at(q)] = x1
        if not last_step:
            for i in range(2):
                khx_s[i] = bdot(left, right3(xhalo_s[step + 1, i]))
                khy_s[i] = bdot(left, right3(yhalo_s[step + 1, i]))
        end_phase(second, 2)
        q_xy = mm(inverse, unpack(second), NT)
        s2 = s_start + c * mm(q_xy, signed[: 4 * rank])
        wide = jnp.concatenate([q_xy, q_z], axis=1)
        q_stack = jnp.concatenate([wide[:, block(i)] for i in range(6)], axis=0)
        ms2 = mm(q_stack, mm(inverse_t, s2))
        mean = jnp.sum(s2 * u_row, axis=1, keepdims=True)
        left = left3(jnp.concatenate([(1.0 - t) * s2, c * ms2], axis=0))
        gram = jnp.zeros((rank, rank), F32)
        for i in range(no // 512):
            here = slice(512 * i, 512 * i + 512)
            out = bdot(left, right3(v_now[:, here]))
            d = d_ref[:, here]
            l1 = out[:rank] + t * mean
            for j, (dim, sign) in enumerate(signs):
                l1 = l1 - (sign * jnp.maximum(sign * d[dim : dim + 1], 0.0)) * out[block(j + 1)]
            v_s[:, here] = l1
            hi, lo = split(l1)
            gram = gram + gram3(hi, lo, hi, lo)
        v_now = v_s
        v_upper, v_inverse = finish(advance(begin(gram * (1.0 / no)), 0, rank // 8))
        if last_step:
            left = left3(v_inverse)
            for i in range(no // 512):
                here = slice(512 * i, 512 * i + 512)
                v_out[:, here] = bdot(left, right3(v_s[:, here]))
            s_out[...] = mm(eye, v_upper, NT)
        else:
            raw_tables, raw_row = tables_of(v_s)
            raw_col = column(raw_row)
            prepare(raw_col)
            prepare_halo(raw_col)
            left = left3(v_inverse)
            wide = mm(v_inverse, raw_tables, NT)
            weights = jnp.concatenate([wide[:, block(i)] for i in range(6)], axis=0)
            u_col = jnp.sum(v_inverse * raw_row, axis=1, keepdims=True)
            u_row = jnp.sum(eye * u_col, axis=0, keepdims=True)
            k_left = left3(v_upper)

            def later(left=left, weights=weights, v_inverse=v_inverse):
                for i in range(no // 512):
                    here = slice(512 * i, 512 * i + 512)
                    v_s[:, here] = bdot(left, right3(v_s[:, here]))
                return mm(weights, v_inverse, NT)

    def drain(a, _):
        for phase in range(3):
            all_of(a, phase, asend).wait()
        return 0

    lax.fori_loop(0, 2 * STEPS, drain, 0)


def store(x_ref, s_ref, v_ref, x_out, s_out, v_out, sems):
    copies = [
        pltpu.make_async_copy(src, dst, sems.at[i])
        for i, (src, dst) in enumerate(((x_ref, x_out), (v_ref, v_out), (s_ref, s_out)))
    ]
    for copy in copies:
        copy.start()
    for copy in copies:
        copy.wait()


def solution(mesh):
    ngx, ngy = mesh.shape["gx"], mesh.shape["gy"]

    def shards(spatial, coupling, orient, directions):
        slabs, ylen, zlen, rank = spatial.shape
        slab = ylen * zlen
        nloc = slabs * slab
        no = orient.shape[0]
        crow = 128 // ngy
        vmem, hbm = pl.BlockSpec(memory_space=pltpu.VMEM), pl.BlockSpec(memory_space=pltpu.HBM)
        sums = 2 * STEPS
        scratch = [
            (nloc, rank), (rank, rank), (rank, no), (3, no),
            (rank, nloc), (rank, nloc), (rank, nloc + slab), (rank, nloc + slab), (4, rank, nloc), (rank, nloc),
            (rank, nloc), (2, rank, slab), (2, rank, 128), (rank, no),
            (STEPS + 1, 2, rank, 128), (STEPS + 1, 2, rank, slab), (STEPS + 1, 2, rank, 128),
            (sums, ngy, crow, 128), (sums, ngy, crow, 128), (sums, crow, 128), (sums, ngx, crow, 128),
            (sums, crow, 128), (sums, ngy, crow, 128), (1, nloc),
        ]
        outs = (
            jax.ShapeDtypeStruct((nloc, rank), F32),
            jax.ShapeDtypeStruct((rank, rank), F32),
            jax.ShapeDtypeStruct((rank, no), F32),
        )
        results = pl.pallas_call(
            functools.partial(kernel, (ngx, ngy, slabs, ylen, zlen)),
            out_shape=outs,
            in_specs=[hbm] * 4,
            out_specs=(vmem, vmem, vmem),
            scratch_shapes=[pltpu.VMEM(shape, F32) for shape in scratch]
            + [
                pltpu.VMEM((3 * rank, nloc + 2 * slab + 256), BF16),
                pltpu.VMEM((2, rank, nloc), BF16),
                pltpu.VMEM((2, rank, nloc), BF16),
                pltpu.SemaphoreType.DMA((slabs + 3,)),
                pltpu.SemaphoreType.DMA((STEPS + 1, 4)),
                pltpu.SemaphoreType.DMA((STEPS + 1, 4)),
                pltpu.SemaphoreType.DMA((sums, 3)),
                pltpu.SemaphoreType.DMA((sums, 3)),
            ],
            compiler_params=pltpu.CompilerParams(
                collective_id=0, has_side_effects=True, vmem_limit_bytes=40 * 1024 * 1024
            ),
        )(*[pltpu.with_memory_space_constraint(a, pltpu.HBM) for a in (spatial.reshape(nloc, rank), coupling, orient.T, directions)])
        x, s, v = pl.pallas_call(
            store,
            out_shape=outs,
            in_specs=[vmem] * 3,
            out_specs=(hbm, hbm, hbm),
            scratch_shapes=[pltpu.SemaphoreType.DMA((3,))],
            compiler_params=pltpu.CompilerParams(vmem_limit_bytes=1024 * 1024),
        )(*results)
        return x.reshape(spatial.shape), s, v.T

    return jax.shard_map(
        shards,
        mesh=mesh,
        in_specs=(P("gx", "gy", None, None), P(), P(), P()),
        out_specs=(P("gx", "gy", None, None), P(), P()),
        check_vma=False,
    )
```

```python
import functools

import jax
import jax.numpy as jnp
from jax import lax
from jax.experimental import pallas as pl
from jax.experimental.pallas import tpu as pltpu
from jax.sharding import PartitionSpec as P

STEPS = 2
MESH = pl.DeviceIdType.MESH
F32 = jnp.float32
BF16 = jnp.bfloat16
NN = (((1,), (0,)), ((), ()))
NT = (((1,), (1,)), ((), ()))

courant = 0.3
tumble = 0.2


def mm(a, b, dims=NN):
    return lax.dot_general(a, b, dims, precision=lax.Precision.HIGHEST, preferred_element_type=F32)


def bdot(a, b, dims=NN):
    return lax.dot_general(a, b, dims, preferred_element_type=F32)


def split(a):
    hi = a.astype(BF16)
    return hi, (a - hi.astype(F32)).astype(BF16)


def left3(a):
    hi, lo = split(a)
    return jnp.concatenate([hi, hi, lo], axis=1)


def right3(b):
    hi, lo = split(b)
    return jnp.concatenate([hi, lo, hi], axis=0)


def mm3(a, b, dims=NN):
    hi, lo = split(b)
    axis = 0 if dims is NN else 1
    return bdot(left3(a), jnp.concatenate([hi, lo, hi], axis=axis), dims)


def gram3(left_hi, left_lo, right_hi, right_lo):
    width = right_hi.shape[0]
    first = bdot(left_hi, jnp.concatenate([right_hi, right_lo], axis=0), NT)
    return first[:, :width] + first[:, width:] + bdot(left_lo, right_hi, NT)


def speed_of(density):
    return 1.0 / (1.0 + density * density)


def begin(gram):
    n = gram.shape[0]
    eye = jnp.where(lax.broadcasted_iota(jnp.int32, (n, n), 0) == lax.broadcasted_iota(jnp.int32, (n, n), 1), 1.0, 0.0)
    both = jnp.concatenate([gram, eye], axis=1)
    return [both[8 * b : 8 * b + 8] for b in range(n // 8)]


def advance(blocks, start, stop):
    width = blocks[0].shape[1]
    below = lax.broadcasted_iota(jnp.int32, (8, width), 0)

    def across(a, c):
        return jnp.broadcast_to(a[:, c : c + 1], (8, width))

    def down(a, r):
        return jnp.broadcast_to(a[r : r + 1], (8, width))

    for kb in range(start, stop):
        own = [across(blocks[kb], 8 * kb + c) for c in range(8)]
        pairs = []
        current = blocks[kb]
        for k in range(0, 8, 2):
            first = {j: down(own[j], k) for j in range(k, 8)}
            second = {j: down(own[j], k + 1) for j in range(k + 1, 8)}
            a, b, d = first[k], first[k + 1], second[k + 1]
            inverse = 1.0 / (a * d - b * b)
            p, q, r = d * inverse, b * inverse, a * inverse
            rows = down(current, k), down(current, k + 1)
            f1 = jnp.where(below > k + 1, own[k] * p - own[k + 1] * q, 0.0)
            f2 = jnp.where(below > k + 1, own[k + 1] * r - own[k] * q, 0.0)
            for j in range(k + 2, 8):
                own[j] = own[j] - f1 * first[j] - f2 * second[j]
            f1 = jnp.where(below == k + 1, b / a, f1)
            current = current - f1 * rows[0] - f2 * rows[1]
            pairs.append((p, q, r, rows, first, second))
        blocks[kb] = current
        for b in range(kb + 1, len(blocks)):
            columns = [across(blocks[b], 8 * kb + c) for c in range(8)]
            for i, (p, q, r, rows, first, second) in enumerate(pairs):
                k = 2 * i
                f1 = columns[k] * p - columns[k + 1] * q
                f2 = columns[k + 1] * r - columns[k] * q
                for j in range(k + 2, 8):
                    columns[j] = columns[j] - f1 * first[j] - f2 * second[j]
                blocks[b] = blocks[b] - f1 * rows[0] - f2 * rows[1]
    return blocks


def finish(blocks):
    whole = jnp.concatenate(blocks, axis=0)
    n = whole.shape[0]
    i, j = (lax.broadcasted_iota(jnp.int32, (n, n), d) for d in range(2))
    diagonal = jnp.sum(jnp.where(i == j, whole[:, :n], 0.0), axis=1, keepdims=True)
    whole = whole * (1.0 / jnp.sqrt(diagonal))
    return jnp.where(j >= i, whole[:, :n], 0.0), whole[:, n:]


def kernel(
    sizes, x_hbm, s_hbm, v_hbm, d_hbm, x_out, s_out, v_out, x_ref, s_ref, v_ref, d_ref,
    k_s, base_s, tpx_s, tmx_s, t_s, k1_s, h_s, khx_s, khy_s, v_s, yface_s,
    xhalo_s, yhalo_s, pay_s, r1_s, c_s, r2_s, f_s, r3_s, den_s, g3_s, kk_s, hh_s,
    isem, hsend, hrecv, asend, arecv,
):
    ngx, ngy, slabs, ylen, zlen = sizes
    slab = ylen * zlen
    nloc = slabs * slab
    cells = float(nloc * ngx * ngy)
    no = v_hbm.shape[1]
    rank = 64
    c, t = courant, tumble
    me_x, me_y = lax.axis_index("gx"), lax.axis_index("gy")
    crow = 128 // ngy
    signs = ((0, 1), (1, 1), (0, -1), (1, -1), (2, 1), (2, -1))

    order = (0, slabs - 1) + tuple(range(1, slabs - 1))
    inputs = [pltpu.make_async_copy(s_hbm, s_ref, isem.at[0])]
    for q in order:
        rows = pl.ds(slab * q, slab)
        inputs.append(pltpu.make_async_copy(x_hbm.at[rows], x_ref.at[rows], isem.at[1 + q]))
    inputs.append(pltpu.make_async_copy(v_hbm, v_ref, isem.at[slabs + 1]))
    inputs.append(pltpu.make_async_copy(d_hbm, d_ref, isem.at[slabs + 2]))
    for copy in inputs:
        copy.start()

    barrier = pltpu.get_barrier_semaphore()

    def greet_x(i, _):
        pl.semaphore_signal(barrier, inc=1, device_id={"gx": lax.rem(me_x + i, ngx), "gy": me_y}, device_id_type=MESH)
        return 0

    def greet_y(i, _):
        pl.semaphore_signal(barrier, inc=1, device_id={"gx": me_x, "gy": lax.rem(me_y + i, ngy)}, device_id_type=MESH)
        return 0

    lax.fori_loop(1, ngx, greet_x, 0)
    lax.fori_loop(1, ngy, greet_y, 0)

    eye = jnp.where(
        lax.broadcasted_iota(jnp.int32, (rank, rank), 0) == lax.broadcasted_iota(jnp.int32, (rank, rank), 1), 1.0, 0.0
    )
    lane = lax.broadcasted_iota(jnp.int32, (rank, 128), 1)
    zpos = lax.rem(lane, zlen)
    group = lane // zlen

    def at(q):
        return slice(slab * q, slab * q + slab)

    def block(i):
        return slice(rank * i, rank * i + rank)

    def cut(a):
        return [a[:, 128 * i : 128 * i + 128] for i in range(a.shape[1] // 128)]

    def roll(a, s):
        s = s % 128
        return a if s == 0 else pltpu.roll(a, s, 1)

    def from_y_before(a, halo=None, q=0):
        last = 0.0 if halo is None else roll(halo, zlen * (-q))
        out = []
        for piece in [roll(piece, zlen) for piece in cut(a)]:
            out.append(jnp.where(lane < zlen, last, piece))
            last = piece
        return jnp.concatenate(out, axis=1)

    def from_y_after(a, halo=None, q=0):
        rolled = [roll(piece, -zlen) for piece in cut(a)]
        rolled.append(0.0 if halo is None else roll(halo, 128 - zlen - zlen * q))
        return jnp.concatenate(
            [jnp.where(lane < 128 - zlen, rolled[i], rolled[i + 1]) for i in range(len(rolled) - 1)], axis=1
        )

    def from_z_before(a):
        return jnp.concatenate([jnp.where(zpos == 0, roll(p, 1 - zlen), roll(p, 1)) for p in cut(a)], axis=1)

    def from_z_after(a):
        return jnp.concatenate([jnp.where(zpos == zlen - 1, roll(p, zlen - 1), roll(p, -1)) for p in cut(a)], axis=1)

    def faces(ref, e):
        first, last = jnp.zeros((rank, 128), F32), jnp.zeros((rank, 128), F32)
        for q in range(slabs):
            low = ref[:, slab * q : slab * q + 128]
            high = ref[:, slab * q + slab - 128 : slab * q + slab]
            first = jnp.where(group == q, roll(low, zlen * q), first)
            last = jnp.where(group == q, roll(high, zlen * q - (128 - zlen)), last)
        yface_s[e, 0] = first
        yface_s[e, 1] = last

    def halo_copies(ref, e):
        left = {"gx": lax.rem(me_x + ngx - 1, ngx), "gy": me_y}
        right = {"gx": lax.rem(me_x + 1, ngx), "gy": me_y}
        under = {"gx": me_x, "gy": lax.rem(me_y + ngy - 1, ngy)}
        over = {"gx": me_x, "gy": lax.rem(me_y + 1, ngy)}
        half = slab // 2
        low, high = pl.ds(0, half), pl.ds(half, half)
        end = nloc - slab
        plan = [
            (ref.at[:, pl.ds(half, half)], xhalo_s.at[e, 1, :, high], left),
            (ref.at[:, pl.ds(end, half)], xhalo_s.at[e, 0, :, low], right),
            (yface_s.at[e, 1], yhalo_s.at[e, 0], over),
            (yface_s.at[e, 0], yhalo_s.at[e, 1], under),
            (ref.at[:, pl.ds(0, half)], xhalo_s.at[e, 1, :, low], left),
            (ref.at[:, pl.ds(end + half, half)], xhalo_s.at[e, 0, :, high], right),
        ]
        return [
            pltpu.make_async_remote_copy(
                src_ref=src, dst_ref=dst, send_sem=hsend.at[e, i], recv_sem=hrecv.at[e, i], device_id=to, device_id_type=MESH
            )
            for i, (src, dst, to) in enumerate(plan)
        ]

    landing = (r1_s, r2_s, r3_s)

    def start_phase(a, phase):
        mine, n = (me_x, ngx) if phase == 1 else (me_y, ngy)
        for i in sorted(range(1, n), key=lambda i: -min(i, n - i)):
            other = lax.rem(mine + i, n)
            pltpu.make_async_remote_copy(
                src_ref=pay_s.at[a, other] if phase == 0 else (c_s if phase == 1 else f_s).at[a],
                dst_ref=landing[phase].at[a, mine],
                send_sem=asend.at[a, phase],
                recv_sem=arecv.at[a, phase],
                device_id={"gx": other, "gy": me_y} if phase == 1 else {"gx": me_x, "gy": other},
                device_id_type=MESH,
            ).start()
        if phase == 0:
            r1_s[a, me_y] = pay_s[a, me_y]
        elif phase == 1:
            r2_s[a, me_x] = c_s[a]
        else:
            r3_s[a, me_y] = f_s[a]

    def all_of(a, phase, sem):
        part = landing[phase].at[a, pl.ds(0, (ngx if phase == 1 else ngy) - 1)]
        return pltpu.make_async_copy(part, part, sem.at[a, phase])

    def end_phase(a, phase):
        all_of(a, phase, arecv).wait()
        if phase == 0:
            c_s[a] = jnp.sum(r1_s[a], axis=0)
        elif phase == 1:
            f_s[a] = jnp.sum(r2_s[a], axis=0)

    def pack(a, raw):
        pay_s[a] = jnp.concatenate([raw[: 2 * rank], raw[2 * rank :]], axis=1).reshape(ngy, crow, 128)

    def unpack(a):
        full = r3_s[a].reshape(128, 128) * (1.0 / cells)
        return jnp.concatenate([full[:, :rank], full[:, rank:]], axis=0)

    def tables_of(ref):
        total = jnp.zeros((6 * rank + 16, rank), F32)
        for i in range(no // 512):
            v = ref[:, 512 * i : 512 * i + 512]
            v_hi, v_lo = split(v)
            d = d_ref[:, 512 * i : 512 * i + 512]
            parts = [v * jnp.maximum(sign * d[dim : dim + 1], 0.0) for dim, sign in signs]
            l_hi, l_lo = split(jnp.concatenate(parts + [jnp.ones((16, 512), F32)], axis=0))
            total = total + gram3(l_hi, l_lo, v_hi, v_lo)
        total = total * (1.0 / no)
        return total[: 6 * rank], total[6 * rank : 6 * rank + 1]

    def column(row):
        return jnp.sum(eye * row, axis=1, keepdims=True)

    def flux(k, u_col):
        density = jnp.sum(k * u_col, axis=0, keepdims=True)
        return density, speed_of(density) * k

    def prepare(u_col):
        for q in range(slabs):
            density, g = flux(k_s[:, at(q)], u_col)
            den_s[:, at(q)] = density
            g3_s[:, at(q)] = right3(g)

    def prepare_halo(u_col):
        for i in range(2):
            g3_s[:, nloc + slab * i : nloc + slab * (i + 1)] = right3(flux(khx_s[i], u_col)[1])
            at_y = nloc + 2 * slab + 128 * i
            g3_s[:, at_y : at_y + 128] = right3(flux(khy_s[i], u_col)[1])

    inputs[0].wait()
    st = left3(mm(eye, s_ref[...], NT))
    first_halo = halo_copies(k_s, 0)
    for i, q in enumerate(order):
        inputs[1 + i].wait()
        x_hi, x_lo = split(x_ref[at(q), :])
        k_s[:, at(q)] = bdot(st[:, :rank], x_hi, NT) + bdot(st[:, rank : 2 * rank], x_lo, NT) + bdot(st[:, 2 * rank :], x_hi, NT)
        if i == 1:
            pl.semaphore_wait(barrier, ngx + ngy - 2)
            for n in (0, 1, 4, 5):
                first_halo[n].start()
    faces(k_s, 0)
    first_halo[2].start()
    first_halo[3].start()
    inputs[slabs + 1].wait()
    inputs[slabs + 2].wait()
    tables, u_row = tables_of(v_ref)
    u_col = column(u_row)
    weights = tables
    prepare(u_col)
    k_left = None
    v_now = v_ref
    later = None

    for step in range(STEPS):
        last_step = step == STEPS - 1
        center = weights[block(0)] + weights[block(1)] + weights[block(2)]
        center = center + weights[block(3)] + weights[block(4)] + weights[block(5)]
        stencil = left3(c * jnp.concatenate([center, weights], axis=0))
        bx = nloc
        by = nloc + 2 * slab

        def halo_terms():
            tpx_s[:, :slab] = bdot(stencil[block(1)], g3_s[:, bx : bx + slab])
            tmx_s[:, slab * slabs :] = bdot(stencil[block(3)], g3_s[:, bx + slab : bx + 2 * slab])
            return (
                bdot(stencil[block(2)], g3_s[:, by : by + 128]),
                bdot(stencil[block(4)], g3_s[:, by + 128 : by + 256]),
            )

        halo = halo_copies(k1_s, step + 1)

        def spread(q):
            k = k_s[:, at(q)]
            if k_left is not None:
                k = bdot(k_left, right3(k))
            out = bdot(stencil, g3_s[:, at(q)])
            base_s[:, at(q)] = (1.0 - t) * k + t * u_col * den_s[:, at(q)] - out[:rank]
            tpx_s[:, at(q + 1)] = out[block(1)]
            t_s[0, :, at(q)] = out[block(2)]
            tmx_s[:, at(q)] = out[block(3)]
            t_s[1, :, at(q)] = out[block(4)]
            t_s[2, :, at(q)] = out[block(5)]
            t_s[3, :, at(q)] = out[block(6)]

        def combine(q):
            k1_s[:, at(q)] = (
                base_s[:, at(q)]
                + tpx_s[:, at(q)]
                + tmx_s[:, at(q + 1)]
                + from_y_before(t_s[0, :, at(q)], tpy, q)
                + from_y_after(t_s[1, :, at(q)], tmy, q)
                + from_z_before(t_s[2, :, at(q)])
                + from_z_after(t_s[3, :, at(q)])
            )

        if step == 0:
            for q in order:
                spread(q)
            for copy in first_halo:
                copy.wait()
            for i in range(2):
                khx_s[i] = xhalo_s[0, i]
                khy_s[i] = yhalo_s[0, i]
            prepare_halo(u_col)
            tpy, tmy = halo_terms()
        else:
            tpy, tmy = halo_terms()
            spread(0)
            spread(1)
        combine(0)
        halo[0].start()
        if step > 0:
            for q in range(slabs - 1, 1, -1):
                spread(q)
        combine(slabs - 1)
        halo[1].start()
        for q in range(1, slabs - 1):
            combine(q)
        faces(k1_s, step + 1)
        halo[2].start()
        halo[3].start()

        first, second = 2 * step, 2 * step + 1
        raw = jnp.zeros((4 * rank, rank), F32)
        for q in range(slabs):
            k1 = k1_s[:, at(q)]
            h = flux(k1, u_col)[1]
            h_s[:, at(q)] = h
            l_hi, l_lo = split(jnp.concatenate([k1, h - from_z_before(h), from_z_after(h) - h, h], axis=0))
            kk_s[0, :, at(q)], kk_s[1, :, at(q)] = l_hi[:rank], l_lo[:rank]
            hh_s[0, :, at(q)], hh_s[1, :, at(q)] = l_hi[3 * rank :], l_lo[3 * rank :]
            raw = raw + gram3(l_hi, l_lo, l_hi[:rank], l_lo[:rank])
        pack(first, raw)
        start_phase(first, 0)
        if not last_step:
            halo[4].start()
            halo[5].start()
        h_k1 = raw[3 * rank :]
        if later is not None:
            tables = later()

        sums = {name: jnp.zeros((rank, rank), F32) for name in ("x-", "y-", "x+", "y+")}
        for q in range(slabs):
            h = h_s[:, at(q)]
            y_hi, y_lo = split(jnp.concatenate([from_y_before(h), from_y_after(h)], axis=0))
            names, his, los = ["y-", "y+"], [y_hi], [y_lo]
            for name, other in (("x-", q - 1), ("x+", q + 1)):
                if 0 <= other < slabs:
                    names.append(name)
                    his.append(hh_s[0, :, at(other)])
                    los.append(hh_s[1, :, at(other)])
            out = gram3(jnp.concatenate(his, axis=0), jnp.concatenate(los, axis=0), kk_s[0, :, at(q)], kk_s[1, :, at(q)])
            for i, name in enumerate(names):
                sums[name] = sums[name] + out[block(i)]
        y_first, y_last = split(yface_s[step + 1, 0]), split(yface_s[step + 1, 1])
        half = slab // 2
        low, high = slice(0, half), slice(half, slab)
        own_low, own_high = slice(0, half), slice(nloc - half, nloc)
        for copy in halo[:4]:
            copy.wait()
        before, after = xhalo_s[step + 1, 0, :, low], xhalo_s[step + 1, 1, :, high]
        b_hi, b_lo = split(before)
        a_hi, a_lo = split(after)
        hb_hi, hb_lo = split(flux(before, u_col)[1])
        ha_hi, ha_lo = split(flux(after, u_col)[1])

        def side(x, y):
            return jnp.concatenate([x, y], axis=1)

        sums["x-"] = sums["x-"] + gram3(
            side(hb_hi, hh_s[0, :, own_high]), side(hb_lo, hh_s[1, :, own_high]),
            side(kk_s[0, :, own_low], a_hi), side(kk_s[1, :, own_low], a_lo),
        )
        sums["x+"] = sums["x+"] + gram3(
            side(hh_s[0, :, own_low], ha_hi), side(hh_s[1, :, own_low], ha_lo),
            side(b_hi, kk_s[0, :, own_high]), side(b_lo, kk_s[1, :, own_high]),
        )
        for i, (name, edge) in enumerate((("y-", y_first), ("y+", y_last))):
            hi, lo = split(flux(yhalo_s[step + 1, i], u_col)[1])
            sums[name] = sums[name] + gram3(hi, lo, *edge)
        pack(
            second,
            jnp.concatenate([h_k1 - sums["x-"], h_k1 - sums["y-"], sums["x+"] - h_k1, sums["y+"] - h_k1], axis=0),
        )
        start_phase(second, 0)
        for phase in range(2):
            for a in (first, second):
                end_phase(a, phase)
                start_phase(a, phase + 1)
        end_phase(first, 2)
        total = unpack(first)
        upper, inverse = finish(advance(begin(total[:rank]), 0, rank // 8))
        inverse_t = mm(eye, inverse, NT)
        q_z = mm3(inverse, total[rank : 3 * rank], NT)
        signed = jnp.concatenate([tables[: 2 * rank], -tables[2 * rank : 4 * rank], tables[block(4)], -tables[block(5)]], axis=0)
        s_start = (1.0 + t) * upper - t * (jnp.sum(upper * u_row, axis=1, keepdims=True) * u_row)
        s_start = s_start + c * mm3(q_z, signed[4 * rank :])
        left = left3(inverse)
        for q in range(slabs):
            x1 = bdot(left, right3(k1_s[:, at(q)]))
            if last_step:
                x_out[at(q), :] = jnp.concatenate([x1, x1], axis=0).T[:, :rank]
            else:
                k_s[:, at(q)] = x1
        if not last_step:
            halo[4].wait()
            halo[5].wait()
            for i in range(2):
                khx_s[i] = bdot(left, right3(xhalo_s[step + 1, i]))
                khy_s[i] = bdot(left, right3(yhalo_s[step + 1, i]))
        end_phase(second, 2)
        q_xy = mm3(inverse, unpack(second), NT)
        s2 = s_start + c * mm3(q_xy, signed[: 4 * rank])
        wide = jnp.concatenate([q_xy, q_z], axis=1)
        q_stack = jnp.concatenate([wide[:, block(i)] for i in range(6)], axis=0)
        ms2 = mm3(q_stack, mm3(inverse_t, s2))
        mean = jnp.sum(s2 * u_row, axis=1, keepdims=True)
        left = left3(jnp.concatenate([(1.0 - t) * s2, c * ms2], axis=0))
        gram = jnp.zeros((rank, rank), F32)
        for i in range(no // 512):
            here = slice(512 * i, 512 * i + 512)
            out = bdot(left, right3(v_now[:, here]))
            d = d_ref[:, here]
            l1 = out[:rank] + t * mean
            for j, (dim, sign) in enumerate(signs):
                l1 = l1 - (sign * jnp.maximum(sign * d[dim : dim + 1], 0.0)) * out[block(j + 1)]
            v_s[:, here] = l1
            hi, lo = split(l1)
            gram = gram + gram3(hi, lo, hi, lo)
        v_now = v_s
        v_upper, v_inverse = finish(advance(begin(gram * (1.0 / no)), 0, rank // 8))
        if last_step:
            left = left3(v_inverse)
            for i in range(no // 512):
                here = slice(512 * i, 512 * i + 512)
                v_out[:, here] = bdot(left, right3(v_s[:, here]))
            s_out[...] = mm(eye, v_upper, NT)
        else:
            raw_tables, raw_row = tables_of(v_s)
            raw_col = column(raw_row)
            prepare(raw_col)
            prepare_halo(raw_col)
            left = left3(v_inverse)
            wide = mm(v_inverse, raw_tables, NT)
            weights = jnp.concatenate([wide[:, block(i)] for i in range(6)], axis=0)
            u_col = jnp.sum(v_inverse * raw_row, axis=1, keepdims=True)
            u_row = jnp.sum(eye * u_col, axis=0, keepdims=True)
            k_left = left3(v_upper)

            def later(left=left, weights=weights, v_inverse=v_inverse):
                for i in range(no // 512):
                    here = slice(512 * i, 512 * i + 512)
                    v_s[:, here] = bdot(left, right3(v_s[:, here]))
                return mm(weights, v_inverse, NT)

    def drain(a, _):
        for phase in range(3):
            all_of(a, phase, asend).wait()
        return 0

    lax.fori_loop(0, 2 * STEPS, drain, 0)


def store(x_ref, s_ref, v_ref, x_out, s_out, v_out, sems):
    copies = [
        pltpu.make_async_copy(src, dst, sems.at[i])
        for i, (src, dst) in enumerate(((x_ref, x_out), (v_ref, v_out), (s_ref, s_out)))
    ]
    for copy in copies:
        copy.start()
    for copy in copies:
        copy.wait()


def solution(mesh):
    ngx, ngy = mesh.shape["gx"], mesh.shape["gy"]

    def shards(spatial, coupling, orient, directions):
        slabs, ylen, zlen, rank = spatial.shape
        slab = ylen * zlen
        nloc = slabs * slab
        no = orient.shape[0]
        crow = 128 // ngy
        vmem, hbm = pl.BlockSpec(memory_space=pltpu.VMEM), pl.BlockSpec(memory_space=pltpu.HBM)
        sums = 2 * STEPS
        scratch = [
            (nloc, rank), (rank, rank), (rank, no), (3, no),
            (rank, nloc), (rank, nloc), (rank, nloc + slab), (rank, nloc + slab), (4, rank, nloc), (rank, nloc),
            (rank, nloc), (2, rank, slab), (2, rank, 128), (rank, no),
            (STEPS + 1, 2, rank, 128), (STEPS + 1, 2, rank, slab), (STEPS + 1, 2, rank, 128),
            (sums, ngy, crow, 128), (sums, ngy, crow, 128), (sums, crow, 128), (sums, ngx, crow, 128),
            (sums, crow, 128), (sums, ngy, crow, 128), (1, nloc),
        ]
        outs = (
            jax.ShapeDtypeStruct((nloc, rank), F32),
            jax.ShapeDtypeStruct((rank, rank), F32),
            jax.ShapeDtypeStruct((rank, no), F32),
        )
        results = pl.pallas_call(
            functools.partial(kernel, (ngx, ngy, slabs, ylen, zlen)),
            out_shape=outs,
            in_specs=[hbm] * 4,
            out_specs=(vmem, vmem, vmem),
            scratch_shapes=[pltpu.VMEM(shape, F32) for shape in scratch]
            + [
                pltpu.VMEM((3 * rank, nloc + 2 * slab + 256), BF16),
                pltpu.VMEM((2, rank, nloc), BF16),
                pltpu.VMEM((2, rank, nloc), BF16),
                pltpu.SemaphoreType.DMA((slabs + 3,)),
                pltpu.SemaphoreType.DMA((STEPS + 1, 6)),
                pltpu.SemaphoreType.DMA((STEPS + 1, 6)),
                pltpu.SemaphoreType.DMA((sums, 3)),
                pltpu.SemaphoreType.DMA((sums, 3)),
            ],
            compiler_params=pltpu.CompilerParams(
                collective_id=0, has_side_effects=True, vmem_limit_bytes=40 * 1024 * 1024
            ),
        )(*[pltpu.with_memory_space_constraint(a, pltpu.HBM) for a in (spatial.reshape(nloc, rank), coupling, orient.T, directions)])
        x, s, v = pl.pallas_call(
            store,
            out_shape=outs,
            in_specs=[vmem] * 3,
            out_specs=(hbm, hbm, hbm),
            scratch_shapes=[pltpu.SemaphoreType.DMA((3,))],
            compiler_params=pltpu.CompilerParams(vmem_limit_bytes=1024 * 1024),
        )(*results)
        return x.reshape(spatial.shape), s, v.T

    return jax.shard_map(
        shards,
        mesh=mesh,
        in_specs=(P("gx", "gy", None, None), P(), P(), P()),
        out_specs=(P("gx", "gy", None, None), P(), P()),
        check_vma=False,
    )
```

```python
import functools

import jax
import jax.numpy as jnp
from jax import lax
from jax.experimental import pallas as pl
from jax.experimental.pallas import tpu as pltpu
from jax.sharding import PartitionSpec as P

STEPS = 2
MESH = pl.DeviceIdType.MESH
F32 = jnp.float32
BF16 = jnp.bfloat16
NN = (((1,), (0,)), ((), ()))
NT = (((1,), (1,)), ((), ()))

courant = 0.3
tumble = 0.2


def mm(a, b, dims=NN):
    return lax.dot_general(a, b, dims, precision=lax.Precision.HIGHEST, preferred_element_type=F32)


def bdot(a, b, dims=NN):
    return lax.dot_general(a, b, dims, preferred_element_type=F32)


def split(a):
    hi = a.astype(BF16)
    return hi, (a - hi.astype(F32)).astype(BF16)


def left3(a):
    hi, lo = split(a)
    return jnp.concatenate([hi, hi, lo], axis=1)


def right3(b):
    hi, lo = split(b)
    return jnp.concatenate([hi, lo, hi], axis=0)


def dot3(a, b, dims=NN):
    return bdot(a[0], b[0], dims) + (bdot(a[0], b[1], dims) + bdot(a[1], b[0], dims))


def mm3(a, b, dims=NN):
    return dot3(split(a), split(b), dims)


def gram3(left_hi, left_lo, right_hi, right_lo):
    width = right_hi.shape[0]
    first = bdot(left_hi, jnp.concatenate([right_hi, right_lo], axis=0), NT)
    return first[:, :width] + first[:, width:] + bdot(left_lo, right_hi, NT)


def speed_of(density):
    return 1.0 / (1.0 + density * density)


def begin(gram):
    n = gram.shape[0]
    eye = jnp.where(lax.broadcasted_iota(jnp.int32, (n, n), 0) == lax.broadcasted_iota(jnp.int32, (n, n), 1), 1.0, 0.0)
    both = jnp.concatenate([gram, eye], axis=1)
    return [both[8 * b : 8 * b + 8] for b in range(n // 8)]


def advance(blocks, start, stop):
    width = blocks[0].shape[1]
    below = lax.broadcasted_iota(jnp.int32, (8, width), 0)

    def across(a, c):
        return jnp.broadcast_to(a[:, c : c + 1], (8, width))

    def down(a, r):
        return jnp.broadcast_to(a[r : r + 1], (8, width))

    count = len(blocks)
    own = [across(blocks[start], 8 * start + c) for c in range(8)]
    for kb in range(start, stop):
        under = {n: [across(blocks[n], 8 * kb + c) for c in range(8)] for n in range(kb + 1, count)}
        ahead = [across(blocks[kb + 1], 8 * kb + 8 + c) for c in range(8)] if kb + 1 < count else None
        current = blocks[kb]
        a, b, d = down(own[0], 0), down(own[1], 0), down(own[1], 1)
        for k in range(0, 8, 2):
            first = {j: down(own[j], k) for j in range(k + 2, 8)}
            second = {j: down(own[j], k + 1) for j in range(k + 2, 8)}
            inverse = 1.0 / (a * d - b * b)
            p, q, r = d * inverse, b * inverse, a * inverse
            ratio = b / a
            if k < 6:
                x0, x1, y0, y1 = down(own[k], k + 2), down(own[k + 1], k + 2), down(own[k], k + 3), down(own[k + 1], k + 3)
                xd, yd = x0 * d - x1 * b, y0 * d - y1 * b
                xa, ya = x1 * a - x0 * b, y1 * a - y0 * b
                a, b, d = (
                    down(own[k + 2], k + 2) - (x0 * xd + x1 * xa) * inverse,
                    down(own[k + 3], k + 2) - (x0 * yd + x1 * ya) * inverse,
                    down(own[k + 3], k + 3) - (y0 * yd + y1 * ya) * inverse,
                )
            rows = down(current, k), down(current, k + 1)
            f1 = jnp.where(below > k + 1, own[k] * p - own[k + 1] * q, 0.0)
            f2 = jnp.where(below > k + 1, own[k + 1] * r - own[k] * q, 0.0)
            for j in range(k + 2, 8):
                own[j] = own[j] - f1 * first[j] - f2 * second[j]
            f1 = jnp.where(below == k + 1, ratio, f1)
            current = current - f1 * rows[0] - f2 * rows[1]
            for n, columns in under.items():
                f1 = columns[k] * p - columns[k + 1] * q
                f2 = columns[k + 1] * r - columns[k] * q
                for j in range(k + 2, 8):
                    columns[j] = columns[j] - f1 * first[j] - f2 * second[j]
                if n == kb + 1:
                    for c in range(8):
                        ahead[c] = ahead[c] - f1 * down(columns[k], c) - f2 * down(columns[k + 1], c)
                blocks[n] = blocks[n] - f1 * rows[0] - f2 * rows[1]
        blocks[kb] = current
        own = ahead
    return blocks


def finish(blocks):
    whole = jnp.concatenate(blocks, axis=0)
    n = whole.shape[0]
    i, j = (lax.broadcasted_iota(jnp.int32, (n, n), d) for d in range(2))
    diagonal = jnp.sum(jnp.where(i == j, whole[:, :n], 0.0), axis=1, keepdims=True)
    whole = whole * (1.0 / jnp.sqrt(diagonal))
    return jnp.where(j >= i, whole[:, :n], 0.0), whole[:, n:]


def kernel(
    sizes, x_hbm, s_hbm, v_hbm, d_hbm, x_out, s_out, v_out, x_ref, s_ref, v_ref, d_ref,
    k_s, base_s, tpx_s, tmx_s, t_s, k1_s, h_s, khx_s, khy_s, v_s, yface_s,
    xhalo_s, yhalo_s, pay_s, r1_s, c_s, r2_s, f_s, r3_s, den_s, g3_s, kk_s, hh_s, v3_s,
    isem, hsend, hrecv, asend, arecv,
):
    ngx, ngy, slabs, ylen, zlen = sizes
    slab = ylen * zlen
    nloc = slabs * slab
    cells = float(nloc * ngx * ngy)
    no = v_hbm.shape[1]
    rank = 64
    c, t = courant, tumble
    me_x, me_y = lax.axis_index("gx"), lax.axis_index("gy")
    crow = 128 // ngy
    signs = ((0, 1), (1, 1), (0, -1), (1, -1), (2, 1), (2, -1))

    order = (0, slabs - 1) + tuple(range(1, slabs - 1))
    inputs = [pltpu.make_async_copy(s_hbm, s_ref, isem.at[0])]
    for q in order:
        rows = pl.ds(slab * q, slab)
        inputs.append(pltpu.make_async_copy(x_hbm.at[rows], x_ref.at[rows], isem.at[1 + q]))
    inputs.append(pltpu.make_async_copy(v_hbm, v_ref, isem.at[slabs + 1]))
    inputs.append(pltpu.make_async_copy(d_hbm, d_ref, isem.at[slabs + 2]))
    for copy in inputs:
        copy.start()

    barrier = pltpu.get_barrier_semaphore()

    def greet_x(i, _):
        pl.semaphore_signal(barrier, inc=1, device_id={"gx": lax.rem(me_x + i, ngx), "gy": me_y}, device_id_type=MESH)
        return 0

    def greet_y(i, _):
        pl.semaphore_signal(barrier, inc=1, device_id={"gx": me_x, "gy": lax.rem(me_y + i, ngy)}, device_id_type=MESH)
        return 0

    lax.fori_loop(1, ngx, greet_x, 0)
    lax.fori_loop(1, ngy, greet_y, 0)

    eye = jnp.where(
        lax.broadcasted_iota(jnp.int32, (rank, rank), 0) == lax.broadcasted_iota(jnp.int32, (rank, rank), 1), 1.0, 0.0
    )
    lane = lax.broadcasted_iota(jnp.int32, (rank, 128), 1)
    zpos = lax.rem(lane, zlen)
    group = lane // zlen

    def at(q):
        return slice(slab * q, slab * q + slab)

    def block(i):
        return slice(rank * i, rank * i + rank)

    def cut(a):
        return [a[:, 128 * i : 128 * i + 128] for i in range(a.shape[1] // 128)]

    def roll(a, s):
        s = s % 128
        return a if s == 0 else pltpu.roll(a, s, 1)

    def from_y_before(a, halo=None, q=0):
        last = 0.0 if halo is None else roll(halo, zlen * (-q))
        out = []
        for piece in [roll(piece, zlen) for piece in cut(a)]:
            out.append(jnp.where(lane < zlen, last, piece))
            last = piece
        return jnp.concatenate(out, axis=1)

    def from_y_after(a, halo=None, q=0):
        rolled = [roll(piece, -zlen) for piece in cut(a)]
        rolled.append(0.0 if halo is None else roll(halo, 128 - zlen - zlen * q))
        return jnp.concatenate(
            [jnp.where(lane < 128 - zlen, rolled[i], rolled[i + 1]) for i in range(len(rolled) - 1)], axis=1
        )

    def from_z_before(a):
        return jnp.concatenate([jnp.where(zpos == 0, roll(p, 1 - zlen), roll(p, 1)) for p in cut(a)], axis=1)

    def from_z_after(a):
        return jnp.concatenate([jnp.where(zpos == zlen - 1, roll(p, zlen - 1), roll(p, -1)) for p in cut(a)], axis=1)

    def faces(ref, e):
        first, last = jnp.zeros((rank, 128), F32), jnp.zeros((rank, 128), F32)
        for q in range(slabs):
            low = ref[:, slab * q : slab * q + 128]
            high = ref[:, slab * q + slab - 128 : slab * q + slab]
            first = jnp.where(group == q, roll(low, zlen * q), first)
            last = jnp.where(group == q, roll(high, zlen * q - (128 - zlen)), last)
        yface_s[e, 0] = first
        yface_s[e, 1] = last

    def halo_copies(ref, e):
        left = {"gx": lax.rem(me_x + ngx - 1, ngx), "gy": me_y}
        right = {"gx": lax.rem(me_x + 1, ngx), "gy": me_y}
        under = {"gx": me_x, "gy": lax.rem(me_y + ngy - 1, ngy)}
        over = {"gx": me_x, "gy": lax.rem(me_y + 1, ngy)}
        half = slab // 2
        low, high = pl.ds(0, half), pl.ds(half, half)
        end = nloc - slab
        plan = [
            (ref.at[:, pl.ds(half, half)], xhalo_s.at[e, 1, :, high], left),
            (ref.at[:, pl.ds(end, half)], xhalo_s.at[e, 0, :, low], right),
            (yface_s.at[e, 1], yhalo_s.at[e, 0], over),
            (yface_s.at[e, 0], yhalo_s.at[e, 1], under),
            (ref.at[:, pl.ds(0, half)], xhalo_s.at[e, 1, :, low], left),
            (ref.at[:, pl.ds(end + half, half)], xhalo_s.at[e, 0, :, high], right),
        ]
        return [
            pltpu.make_async_remote_copy(
                src_ref=src, dst_ref=dst, send_sem=hsend.at[e, i], recv_sem=hrecv.at[e, i], device_id=to, device_id_type=MESH
            )
            for i, (src, dst, to) in enumerate(plan)
        ]

    landing = (r1_s, r2_s, r3_s)

    def start_phase(a, phase):
        mine, n = (me_x, ngx) if phase == 1 else (me_y, ngy)
        for i in sorted(range(1, n), key=lambda i: -min(i, n - i)):
            other = lax.rem(mine + i, n)
            pltpu.make_async_remote_copy(
                src_ref=pay_s.at[a, other] if phase == 0 else (c_s if phase == 1 else f_s).at[a],
                dst_ref=landing[phase].at[a, mine],
                send_sem=asend.at[a, phase],
                recv_sem=arecv.at[a, phase],
                device_id={"gx": other, "gy": me_y} if phase == 1 else {"gx": me_x, "gy": other},
                device_id_type=MESH,
            ).start()
        if phase == 0:
            r1_s[a, me_y] = pay_s[a, me_y]
        elif phase == 1:
            r2_s[a, me_x] = c_s[a]
        else:
            r3_s[a, me_y] = f_s[a]

    def all_of(a, phase, sem):
        part = landing[phase].at[a, pl.ds(0, (ngx if phase == 1 else ngy) - 1)]
        return pltpu.make_async_copy(part, part, sem.at[a, phase])

    def end_phase(a, phase):
        all_of(a, phase, arecv).wait()
        if phase == 0:
            c_s[a] = jnp.sum(r1_s[a], axis=0)
        elif phase == 1:
            f_s[a] = jnp.sum(r2_s[a], axis=0)

    def pack(a, raw):
        pay_s[a] = jnp.concatenate([raw[: 2 * rank], raw[2 * rank :]], axis=1).reshape(ngy, crow, 128)

    def unpack(a):
        full = r3_s[a].reshape(128, 128) * (1.0 / cells)
        return jnp.concatenate([full[:, :rank], full[:, rank:]], axis=0)

    def tables_of(ref):
        total = jnp.zeros((6 * rank + 16, rank), F32)
        for i in range(no // 512):
            v = ref[:, 512 * i : 512 * i + 512]
            v_hi, v_lo = split(v)
            d = d_ref[:, 512 * i : 512 * i + 512]
            parts = [v * jnp.maximum(sign * d[dim : dim + 1], 0.0) for dim, sign in signs]
            l_hi, l_lo = split(jnp.concatenate(parts + [jnp.ones((16, 512), F32)], axis=0))
            total = total + gram3(l_hi, l_lo, v_hi, v_lo)
        total = total * (1.0 / no)
        return total[: 6 * rank], total[6 * rank : 6 * rank + 1]

    def column(row):
        return jnp.sum(eye * row, axis=1, keepdims=True)

    half_lane = lax.broadcasted_iota(jnp.int32, (3 * rank, 128), 1) < rank

    def doubled(a):
        hi, lo = split(a)
        return jnp.concatenate([hi, lo[:, :rank]], axis=1)

    def pair_left(first, a):
        turned = pltpu.roll(a, rank, 1)
        return jnp.concatenate(
            [doubled(first), doubled(jnp.where(half_lane, a, turned)), doubled(jnp.where(half_lane, turned, a))], axis=0
        )

    def place(j):
        return block(1 + j // 2 + 3 * (j % 2))

    def flux(k, u_col):
        density = jnp.sum(k * u_col, axis=0, keepdims=True)
        return density, speed_of(density) * k

    def prepare(u_col):
        for q in range(slabs):
            density, g = flux(k_s[:, at(q)], u_col)
            den_s[:, at(q)] = density
            g3_s[:, at(q)] = right3(g)

    def prepare_halo(u_col):
        for i in range(2):
            g3_s[:, nloc + slab * i : nloc + slab * (i + 1)] = right3(flux(khx_s[i], u_col)[1])
            at_y = nloc + 2 * slab + 128 * i
            g3_s[:, at_y : at_y + 128] = right3(flux(khy_s[i], u_col)[1])

    inputs[0].wait()
    st = left3(mm(eye, s_ref[...], NT))
    first_halo = halo_copies(k_s, 0)
    for i, q in enumerate(order):
        inputs[1 + i].wait()
        x_hi, x_lo = split(x_ref[at(q), :])
        k_s[:, at(q)] = bdot(st[:, :rank], x_hi, NT) + bdot(st[:, rank : 2 * rank], x_lo, NT) + bdot(st[:, 2 * rank :], x_hi, NT)
        if i == 1:
            pl.semaphore_wait(barrier, ngx + ngy - 2)
            for n in (0, 1, 4, 5):
                first_halo[n].start()
    faces(k_s, 0)
    first_halo[2].start()
    first_halo[3].start()
    inputs[slabs + 1].wait()
    inputs[slabs + 2].wait()
    tables, u_row = tables_of(v_ref)
    u_col = column(u_row)
    wide = None
    prepare(u_col)
    k_left = None
    v_now = v_ref
    later = None

    for step in range(STEPS):
        last_step = step == STEPS - 1
        if step == 0:
            center = sum(tables[block(i)] for i in range(1, 6)) + tables[block(0)]
            stencil = left3(c * jnp.concatenate([center] + [tables[block(i)] for i in (0, 2, 4, 1, 3, 5)], axis=0))
        else:
            center = wide[:, :128] + wide[:, 128:256] + wide[:, 256:]
            weights = jnp.concatenate([wide[:, 128 * i : 128 * i + 128] for i in range(3)], axis=0)
            stencil = pair_left(c * (center + pltpu.roll(center, rank, 1)), c * weights)
        bx = nloc
        by = nloc + 2 * slab

        def halo_terms():
            tpx_s[:, :slab] = bdot(stencil[place(0)], g3_s[:, bx : bx + slab])
            tmx_s[:, slab * slabs :] = bdot(stencil[place(2)], g3_s[:, bx + slab : bx + 2 * slab])
            return (
                bdot(stencil[place(1)], g3_s[:, by : by + 128]),
                bdot(stencil[place(3)], g3_s[:, by + 128 : by + 256]),
            )

        halo = halo_copies(k1_s, step + 1)

        def spread(q):
            k = k_s[:, at(q)]
            if k_left is not None:
                k = bdot(k_left, right3(k))
            out = bdot(stencil, g3_s[:, at(q)])
            base_s[:, at(q)] = (1.0 - t) * k + t * u_col * den_s[:, at(q)] - out[:rank]
            tpx_s[:, at(q + 1)] = out[place(0)]
            t_s[0, :, at(q)] = out[place(1)]
            tmx_s[:, at(q)] = out[place(2)]
            t_s[1, :, at(q)] = out[place(3)]
            t_s[2, :, at(q)] = out[place(4)]
            t_s[3, :, at(q)] = out[place(5)]

        def combine(q):
            k1_s[:, at(q)] = (
                base_s[:, at(q)]
                + tpx_s[:, at(q)]
                + tmx_s[:, at(q + 1)]
                + from_y_before(t_s[0, :, at(q)], tpy, q)
                + from_y_after(t_s[1, :, at(q)], tmy, q)
                + from_z_before(t_s[2, :, at(q)])
                + from_z_after(t_s[3, :, at(q)])
            )

        if step == 0:
            for q in order:
                spread(q)
            for copy in first_halo:
                copy.wait()
            for i in range(2):
                khx_s[i] = xhalo_s[0, i]
                khy_s[i] = yhalo_s[0, i]
            prepare_halo(u_col)
            tpy, tmy = halo_terms()
        else:
            tpy, tmy = halo_terms()
            spread(0)
            spread(1)
        combine(0)
        halo[0].start()
        if step > 0:
            for q in range(slabs - 1, 1, -1):
                spread(q)
        combine(slabs - 1)
        halo[1].start()
        for q in range(1, slabs - 1):
            combine(q)
        faces(k1_s, step + 1)
        halo[2].start()
        halo[3].start()

        first, second = 2 * step, 2 * step + 1
        raw = jnp.zeros((4 * rank, rank), F32)
        for q in range(slabs):
            k1 = k1_s[:, at(q)]
            h = flux(k1, u_col)[1]
            h_s[:, at(q)] = h
            l_hi, l_lo = split(jnp.concatenate([k1, h - from_z_before(h), from_z_after(h) - h, h], axis=0))
            kk_s[0, :, at(q)], kk_s[1, :, at(q)] = l_hi[:rank], l_lo[:rank]
            hh_s[0, :, at(q)], hh_s[1, :, at(q)] = l_hi[3 * rank :], l_lo[3 * rank :]
            raw = raw + gram3(l_hi, l_lo, l_hi[:rank], l_lo[:rank])
        pack(first, raw)
        start_phase(first, 0)
        if not last_step:
            halo[4].start()
            halo[5].start()
        h_k1 = raw[3 * rank :]
        if later is not None:
            tables = later()

        sums = {name: jnp.zeros((rank, rank), F32) for name in ("x-", "y-", "x+", "y+")}
        for q in range(slabs):
            h = h_s[:, at(q)]
            y_hi, y_lo = split(jnp.concatenate([from_y_before(h), from_y_after(h)], axis=0))
            names, his, los = ["y-", "y+"], [y_hi], [y_lo]
            for name, other in (("x-", q - 1), ("x+", q + 1)):
                if 0 <= other < slabs:
                    names.append(name)
                    his.append(hh_s[0, :, at(other)])
                    los.append(hh_s[1, :, at(other)])
            out = gram3(jnp.concatenate(his, axis=0), jnp.concatenate(los, axis=0), kk_s[0, :, at(q)], kk_s[1, :, at(q)])
            for i, name in enumerate(names):
                sums[name] = sums[name] + out[block(i)]
        y_first, y_last = split(yface_s[step + 1, 0]), split(yface_s[step + 1, 1])
        half = slab // 2
        low, high = slice(0, half), slice(half, slab)
        own_low, own_high = slice(0, half), slice(nloc - half, nloc)
        for copy in halo[:4]:
            copy.wait()
        before, after = xhalo_s[step + 1, 0, :, low], xhalo_s[step + 1, 1, :, high]
        b_hi, b_lo = split(before)
        a_hi, a_lo = split(after)
        hb_hi, hb_lo = split(flux(before, u_col)[1])
        ha_hi, ha_lo = split(flux(after, u_col)[1])

        def side(x, y):
            return jnp.concatenate([x, y], axis=1)

        sums["x-"] = sums["x-"] + gram3(
            side(hb_hi, hh_s[0, :, own_high]), side(hb_lo, hh_s[1, :, own_high]),
            side(kk_s[0, :, own_low], a_hi), side(kk_s[1, :, own_low], a_lo),
        )
        sums["x+"] = sums["x+"] + gram3(
            side(hh_s[0, :, own_low], ha_hi), side(hh_s[1, :, own_low], ha_lo),
            side(b_hi, kk_s[0, :, own_high]), side(b_lo, kk_s[1, :, own_high]),
        )
        for i, (name, edge) in enumerate((("y-", y_first), ("y+", y_last))):
            hi, lo = split(flux(yhalo_s[step + 1, i], u_col)[1])
            sums[name] = sums[name] + gram3(hi, lo, *edge)
        pack(
            second,
            jnp.concatenate([h_k1 - sums["x-"], h_k1 - sums["y-"], sums["x+"] - h_k1, sums["y+"] - h_k1], axis=0),
        )
        start_phase(second, 0)
        for i in range(no // 512):
            here = slice(512 * i, 512 * i + 512)
            v3_s[:, here] = right3(v_now[:, here])
        for phase in range(2):
            for a in (first, second):
                end_phase(a, phase)
                start_phase(a, phase + 1)
        end_phase(first, 2)
        total = unpack(first)
        upper, inverse = finish(advance(begin(total[:rank]), 0, rank // 8))
        none = jnp.zeros((rank, rank), F32)

        def twice(a):
            return jnp.concatenate(
                [jnp.concatenate([a, none], axis=1), jnp.concatenate([none, a], axis=1)], axis=0
            )

        inverse_2, inverse_t = split(twice(inverse)), split(twice(mm(eye, inverse, NT)))
        q_z = mm3(inverse, total[rank : 3 * rank], NT)
        m_z = dot3(split(q_z), inverse_t)
        signed = jnp.concatenate([tables[: 2 * rank], -tables[2 * rank : 4 * rank], tables[block(4)], -tables[block(5)]], axis=0)
        signed = jnp.concatenate([signed, signed], axis=1)
        s_start = (1.0 + t) * upper - t * (jnp.sum(upper * u_row, axis=1, keepdims=True) * u_row)
        s_start = jnp.concatenate([s_start, s_start], axis=1) + c * mm3(q_z, signed[4 * rank :])
        signed = split(c * signed[: 4 * rank])
        left = left_x = left3(inverse)
        if not last_step:
            for q in range(slabs):
                k_s[:, at(q)] = bdot(left, right3(k1_s[:, at(q)]))
        if not last_step:
            halo[4].wait()
            halo[5].wait()
            for i in range(2):
                khx_s[i] = bdot(left, right3(xhalo_s[step + 1, i]))
                khy_s[i] = bdot(left, right3(yhalo_s[step + 1, i]))
        end_phase(second, 2)
        both = split(dot3(inverse_2, split(r3_s[second].reshape(128, 128) * (1.0 / cells)), NT))
        m_all = jnp.concatenate([dot3(both, inverse_t), m_z], axis=0)
        s2 = s_start + dot3([x[:rank] for x in both], [x[: 2 * rank] for x in signed])
        s2 = s2 + dot3([x[rank:] for x in both], [x[2 * rank :] for x in signed])
        s2_2 = jnp.concatenate([jnp.where(half_lane[:rank], s2, 0.0), jnp.where(half_lane[:rank], 0.0, s2)], axis=0)
        ms2 = mm3(m_all, s2_2)
        mean = jnp.sum(s2[:, :rank] * u_row, axis=1, keepdims=True)
        left = pair_left((1.0 - t) * s2, c * ms2)
        gram = jnp.zeros((rank, rank), F32)
        for i in range(no // 512):
            here = slice(512 * i, 512 * i + 512)
            out = bdot(left, v3_s[:, here])
            d = d_ref[:, here]
            l1 = out[:rank] + t * mean
            for j, (dim, sign) in enumerate(signs):
                l1 = l1 - (sign * jnp.maximum(sign * d[dim : dim + 1], 0.0)) * out[place(j)]
            v_s[:, here] = l1
            hi, lo = split(l1)
            gram = gram + gram3(hi, lo, hi, lo)
        v_now = v_s
        v_upper, v_inverse = finish(advance(begin(gram * (1.0 / no)), 0, rank // 8))
        if last_step:
            for q in range(slabs):
                x1 = bdot(left_x, right3(k1_s[:, at(q)]))
                x_out[at(q), :] = jnp.concatenate([x1, x1], axis=0).T[:, :rank]
            left = left3(v_inverse)
            for i in range(no // 512):
                here = slice(512 * i, 512 * i + 512)
                v_out[:, here] = bdot(left, right3(v_s[:, here]))
            s_out[...] = mm(eye, v_upper, NT)
        else:
            raw_tables, raw_row = tables_of(v_s)
            table_parts = split(raw_tables)
            raw_col = column(raw_row)
            prepare(raw_col)
            prepare_halo(raw_col)
            left = left3(v_inverse)
            wide = dot3(split(v_inverse), table_parts, NT)
            u_col = jnp.sum(v_inverse * raw_row, axis=1, keepdims=True)
            u_row = jnp.sum(eye * u_col, axis=0, keepdims=True)
            k_left = left3(v_upper)

            def later(left=left, wide=wide, v_inverse=v_inverse):
                for i in range(no // 512):
                    here = slice(512 * i, 512 * i + 512)
                    v_s[:, here] = bdot(left, right3(v_s[:, here]))
                return mm(jnp.concatenate([wide[:, block(i)] for i in range(6)], axis=0), v_inverse, NT)

    def drain(a, _):
        for phase in range(3):
            all_of(a, phase, asend).wait()
        return 0

    lax.fori_loop(0, 2 * STEPS, drain, 0)


def store(x_ref, s_ref, v_ref, x_out, s_out, v_out, sems):
    copies = [
        pltpu.make_async_copy(src, dst, sems.at[i])
        for i, (src, dst) in enumerate(((x_ref, x_out), (v_ref, v_out), (s_ref, s_out)))
    ]
    for copy in copies:
        copy.start()
    for copy in copies:
        copy.wait()


def solution(mesh):
    ngx, ngy = mesh.shape["gx"], mesh.shape["gy"]

    def shards(spatial, coupling, orient, directions):
        slabs, ylen, zlen, rank = spatial.shape
        slab = ylen * zlen
        nloc = slabs * slab
        no = orient.shape[0]
        crow = 128 // ngy
        vmem, hbm = pl.BlockSpec(memory_space=pltpu.VMEM), pl.BlockSpec(memory_space=pltpu.HBM)
        sums = 2 * STEPS
        scratch = [
            (nloc, rank), (rank, rank), (rank, no), (3, no),
            (rank, nloc), (rank, nloc), (rank, nloc + slab), (rank, nloc + slab), (4, rank, nloc), (rank, nloc),
            (rank, nloc), (2, rank, slab), (2, rank, 128), (rank, no),
            (STEPS + 1, 2, rank, 128), (STEPS + 1, 2, rank, slab), (STEPS + 1, 2, rank, 128),
            (sums, ngy, crow, 128), (sums, ngy, crow, 128), (sums, crow, 128), (sums, ngx, crow, 128),
            (sums, crow, 128), (sums, ngy, crow, 128), (1, nloc),
        ]
        outs = (
            jax.ShapeDtypeStruct((nloc, rank), F32),
            jax.ShapeDtypeStruct((rank, rank), F32),
            jax.ShapeDtypeStruct((rank, no), F32),
        )
        results = pl.pallas_call(
            functools.partial(kernel, (ngx, ngy, slabs, ylen, zlen)),
            out_shape=outs,
            in_specs=[hbm] * 4,
            out_specs=(vmem, vmem, vmem),
            scratch_shapes=[pltpu.VMEM(shape, F32) for shape in scratch]
            + [
                pltpu.VMEM((3 * rank, nloc + 2 * slab + 256), BF16),
                pltpu.VMEM((2, rank, nloc), BF16),
                pltpu.VMEM((2, rank, nloc), BF16),
                pltpu.VMEM((3 * rank, no), BF16),
                pltpu.SemaphoreType.DMA((slabs + 3,)),
                pltpu.SemaphoreType.DMA((STEPS + 1, 6)),
                pltpu.SemaphoreType.DMA((STEPS + 1, 6)),
                pltpu.SemaphoreType.DMA((sums, 3)),
                pltpu.SemaphoreType.DMA((sums, 3)),
            ],
            compiler_params=pltpu.CompilerParams(
                collective_id=0, has_side_effects=True, vmem_limit_bytes=40 * 1024 * 1024
            ),
        )(*[pltpu.with_memory_space_constraint(a, pltpu.HBM) for a in (spatial.reshape(nloc, rank), coupling, orient.T, directions)])
        x, s, v = pl.pallas_call(
            store,
            out_shape=outs,
            in_specs=[vmem] * 3,
            out_specs=(hbm, hbm, hbm),
            scratch_shapes=[pltpu.SemaphoreType.DMA((3,))],
            compiler_params=pltpu.CompilerParams(vmem_limit_bytes=1024 * 1024),
        )(*results)
        return x.reshape(spatial.shape), s, v.T

    return jax.shard_map(
        shards,
        mesh=mesh,
        in_specs=(P("gx", "gy", None, None), P(), P(), P()),
        out_specs=(P("gx", "gy", None, None), P(), P()),
        check_vma=False,
    )
```

```python
import functools

import jax
import jax.numpy as jnp
from jax import lax
from jax.experimental import pallas as pl
from jax.experimental.pallas import tpu as pltpu
from jax.sharding import PartitionSpec as P

STEPS = 2
MESH = pl.DeviceIdType.MESH
F32 = jnp.float32
BF16 = jnp.bfloat16
NN = (((1,), (0,)), ((), ()))
NT = (((1,), (1,)), ((), ()))

courant = 0.3
tumble = 0.2


def mm(a, b, dims=NN):
    return lax.dot_general(a, b, dims, precision=lax.Precision.HIGHEST, preferred_element_type=F32)


def bdot(a, b, dims=NN):
    return lax.dot_general(a, b, dims, preferred_element_type=F32)


def split(a):
    hi = a.astype(BF16)
    return hi, (a - hi.astype(F32)).astype(BF16)


def left3(a):
    hi, lo = split(a)
    return jnp.concatenate([hi, hi, lo], axis=1)


def right3(b):
    hi, lo = split(b)
    return jnp.concatenate([hi, lo, hi], axis=0)


def dot3(a, b, dims=NN):
    return bdot(a[0], b[0], dims) + (bdot(a[0], b[1], dims) + bdot(a[1], b[0], dims))


def mm3(a, b, dims=NN):
    return dot3(split(a), split(b), dims)


def gram3(left_hi, left_lo, right_hi, right_lo):
    width = right_hi.shape[0]
    first = bdot(left_hi, jnp.concatenate([right_hi, right_lo], axis=0), NT)
    return first[:, :width] + first[:, width:] + bdot(left_lo, right_hi, NT)


def speed_of(density):
    return 1.0 / (1.0 + density * density)


def begin(gram):
    n = gram.shape[0]
    eye = jnp.where(lax.broadcasted_iota(jnp.int32, (n, n), 0) == lax.broadcasted_iota(jnp.int32, (n, n), 1), 1.0, 0.0)
    both = jnp.concatenate([gram, eye], axis=1)
    return [both[8 * b : 8 * b + 8] for b in range(n // 8)]


def advance(blocks, start, stop):
    width = blocks[0].shape[1]
    below = lax.broadcasted_iota(jnp.int32, (8, width), 0)

    def across(a, c):
        return jnp.broadcast_to(a[:, c : c + 1], (8, width))

    def down(a, r):
        return jnp.broadcast_to(a[r : r + 1], (8, width))

    count = len(blocks)
    own = [across(blocks[start], 8 * start + c) for c in range(8)]
    for kb in range(start, stop):
        under = {n: [across(blocks[n], 8 * kb + c) for c in range(8)] for n in range(kb + 1, count)}
        ahead = [across(blocks[kb + 1], 8 * kb + 8 + c) for c in range(8)] if kb + 1 < count else None
        current = blocks[kb]
        a, b, d = down(own[0], 0), down(own[1], 0), down(own[1], 1)
        for k in range(0, 8, 2):
            first = {j: down(own[j], k) for j in range(k + 2, 8)}
            second = {j: down(own[j], k + 1) for j in range(k + 2, 8)}
            inverse = 1.0 / (a * d - b * b)
            p, q, r = d * inverse, b * inverse, a * inverse
            ratio = b / a
            if k < 6:
                x0, x1, y0, y1 = down(own[k], k + 2), down(own[k + 1], k + 2), down(own[k], k + 3), down(own[k + 1], k + 3)
                xd, yd = x0 * d - x1 * b, y0 * d - y1 * b
                xa, ya = x1 * a - x0 * b, y1 * a - y0 * b
                a, b, d = (
                    down(own[k + 2], k + 2) - (x0 * xd + x1 * xa) * inverse,
                    down(own[k + 3], k + 2) - (x0 * yd + x1 * ya) * inverse,
                    down(own[k + 3], k + 3) - (y0 * yd + y1 * ya) * inverse,
                )
            rows = down(current, k), down(current, k + 1)
            f1 = jnp.where(below > k + 1, own[k] * p - own[k + 1] * q, 0.0)
            f2 = jnp.where(below > k + 1, own[k + 1] * r - own[k] * q, 0.0)
            for j in range(k + 2, 8):
                own[j] = own[j] - f1 * first[j] - f2 * second[j]
            f1 = jnp.where(below == k + 1, ratio, f1)
            current = current - f1 * rows[0] - f2 * rows[1]
            for n, columns in under.items():
                f1 = columns[k] * p - columns[k + 1] * q
                f2 = columns[k + 1] * r - columns[k] * q
                for j in range(k + 2, 8):
                    columns[j] = columns[j] - f1 * first[j] - f2 * second[j]
                if n == kb + 1:
                    for c in range(8):
                        ahead[c] = ahead[c] - f1 * down(columns[k], c) - f2 * down(columns[k + 1], c)
                blocks[n] = blocks[n] - f1 * rows[0] - f2 * rows[1]
        blocks[kb] = current
        own = ahead
    return blocks


def finish(blocks):
    whole = jnp.concatenate(blocks, axis=0)
    n = whole.shape[0]
    i, j = (lax.broadcasted_iota(jnp.int32, (n, n), d) for d in range(2))
    diagonal = jnp.sum(jnp.where(i == j, whole[:, :n], 0.0), axis=1, keepdims=True)
    whole = whole * (1.0 / jnp.sqrt(diagonal))
    return jnp.where(j >= i, whole[:, :n], 0.0), whole[:, n:]


def kernel(
    sizes, x_hbm, s_hbm, v_hbm, d_hbm, x_out, s_out, v_out, x_ref, s_ref, v_ref, d_ref,
    k_s, base_s, tpx_s, tmx_s, t_s, k1_s, h_s, khx_s, khy_s, v_s, yface_s,
    xhalo_s, yhalo_s, pay_s, r1_s, c_s, r2_s, f_s, r3_s, den_s, g3_s, kk_s, hh_s, v3_s,
    isem, hsend, hrecv, asend, arecv,
):
    ngx, ngy, slabs, ylen, zlen = sizes
    slab = ylen * zlen
    nloc = slabs * slab
    cells = float(nloc * ngx * ngy)
    no = v_hbm.shape[1]
    rank = 64
    c, t = courant, tumble
    me_x, me_y = lax.axis_index("gx"), lax.axis_index("gy")
    crow = 128 // ngy
    signs = ((0, 1), (1, 1), (0, -1), (1, -1), (2, 1), (2, -1))

    order = (0, slabs - 1) + tuple(range(1, slabs - 1))
    inputs = [pltpu.make_async_copy(s_hbm, s_ref, isem.at[0])]
    for q in order:
        rows = pl.ds(slab * q, slab)
        inputs.append(pltpu.make_async_copy(x_hbm.at[rows], x_ref.at[rows], isem.at[1 + q]))
    inputs.append(pltpu.make_async_copy(v_hbm, v_ref, isem.at[slabs + 1]))
    inputs.append(pltpu.make_async_copy(d_hbm, d_ref, isem.at[slabs + 2]))
    for copy in inputs:
        copy.start()

    barrier = pltpu.get_barrier_semaphore()

    def greet_x(i, _):
        pl.semaphore_signal(barrier, inc=1, device_id={"gx": lax.rem(me_x + i, ngx), "gy": me_y}, device_id_type=MESH)
        return 0

    def greet_y(i, _):
        pl.semaphore_signal(barrier, inc=1, device_id={"gx": me_x, "gy": lax.rem(me_y + i, ngy)}, device_id_type=MESH)
        return 0

    lax.fori_loop(1, ngx, greet_x, 0)
    lax.fori_loop(1, ngy, greet_y, 0)

    eye = jnp.where(
        lax.broadcasted_iota(jnp.int32, (rank, rank), 0) == lax.broadcasted_iota(jnp.int32, (rank, rank), 1), 1.0, 0.0
    )
    lane = lax.broadcasted_iota(jnp.int32, (rank, 128), 1)
    zpos = lax.rem(lane, zlen)
    group = lane // zlen

    def at(q):
        return slice(slab * q, slab * q + slab)

    def block(i):
        return slice(rank * i, rank * i + rank)

    def cut(a):
        return [a[:, 128 * i : 128 * i + 128] for i in range(a.shape[1] // 128)]

    def roll(a, s):
        s = s % 128
        return a if s == 0 else pltpu.roll(a, s, 1)

    def from_y_before(a, halo=None, q=0):
        last = 0.0 if halo is None else roll(halo, zlen * (-q))
        out = []
        for piece in [roll(piece, zlen) for piece in cut(a)]:
            out.append(jnp.where(lane < zlen, last, piece))
            last = piece
        return jnp.concatenate(out, axis=1)

    def from_y_after(a, halo=None, q=0):
        rolled = [roll(piece, -zlen) for piece in cut(a)]
        rolled.append(0.0 if halo is None else roll(halo, 128 - zlen - zlen * q))
        return jnp.concatenate(
            [jnp.where(lane < 128 - zlen, rolled[i], rolled[i + 1]) for i in range(len(rolled) - 1)], axis=1
        )

    def from_z_before(a):
        return jnp.concatenate([jnp.where(zpos == 0, roll(p, 1 - zlen), roll(p, 1)) for p in cut(a)], axis=1)

    def from_z_after(a):
        return jnp.concatenate([jnp.where(zpos == zlen - 1, roll(p, zlen - 1), roll(p, -1)) for p in cut(a)], axis=1)

    def faces(ref, e):
        first, last = jnp.zeros((rank, 128), F32), jnp.zeros((rank, 128), F32)
        for q in range(slabs):
            low = ref[:, slab * q : slab * q + 128]
            high = ref[:, slab * q + slab - 128 : slab * q + slab]
            first = jnp.where(group == q, roll(low, zlen * q), first)
            last = jnp.where(group == q, roll(high, zlen * q - (128 - zlen)), last)
        yface_s[e, 0] = first
        yface_s[e, 1] = last

    def halo_copies(ref, e):
        left = {"gx": lax.rem(me_x + ngx - 1, ngx), "gy": me_y}
        right = {"gx": lax.rem(me_x + 1, ngx), "gy": me_y}
        under = {"gx": me_x, "gy": lax.rem(me_y + ngy - 1, ngy)}
        over = {"gx": me_x, "gy": lax.rem(me_y + 1, ngy)}
        half = slab // 2
        low, high = pl.ds(0, half), pl.ds(half, half)
        end = nloc - slab
        plan = [
            (ref.at[:, pl.ds(half, half)], xhalo_s.at[e, 1, :, high], left),
            (ref.at[:, pl.ds(end, half)], xhalo_s.at[e, 0, :, low], right),
            (yface_s.at[e, 1], yhalo_s.at[e, 0], over),
            (yface_s.at[e, 0], yhalo_s.at[e, 1], under),
            (ref.at[:, pl.ds(0, half)], xhalo_s.at[e, 1, :, low], left),
            (ref.at[:, pl.ds(end + half, half)], xhalo_s.at[e, 0, :, high], right),
        ]
        return [
            pltpu.make_async_remote_copy(
                src_ref=src, dst_ref=dst, send_sem=hsend.at[e, i], recv_sem=hrecv.at[e, i], device_id=to, device_id_type=MESH
            )
            for i, (src, dst, to) in enumerate(plan)
        ]

    landing = (r1_s, r2_s, r3_s)

    def start_phase(a, phase):
        mine, n = (me_x, ngx) if phase == 1 else (me_y, ngy)
        for i in sorted(range(1, n), key=lambda i: -min(i, n - i)):
            other = lax.rem(mine + i, n)
            pltpu.make_async_remote_copy(
                src_ref=pay_s.at[a, other] if phase == 0 else (c_s if phase == 1 else f_s).at[a],
                dst_ref=landing[phase].at[a, mine],
                send_sem=asend.at[a, phase],
                recv_sem=arecv.at[a, phase],
                device_id={"gx": other, "gy": me_y} if phase == 1 else {"gx": me_x, "gy": other},
                device_id_type=MESH,
            ).start()
        if phase == 0:
            r1_s[a, me_y] = pay_s[a, me_y]
        elif phase == 1:
            r2_s[a, me_x] = c_s[a]
        else:
            r3_s[a, me_y] = f_s[a]

    def all_of(a, phase, sem):
        part = landing[phase].at[a, pl.ds(0, (ngx if phase == 1 else ngy) - 1)]
        return pltpu.make_async_copy(part, part, sem.at[a, phase])

    def end_phase(a, phase):
        all_of(a, phase, arecv).wait()
        if phase == 0:
            c_s[a] = jnp.sum(r1_s[a], axis=0)
        elif phase == 1:
            f_s[a] = jnp.sum(r2_s[a], axis=0)

    def pack(a, raw):
        pay_s[a] = jnp.concatenate([raw[: 2 * rank], raw[2 * rank :]], axis=1).reshape(ngy, crow, 128)

    def unpack(a):
        full = r3_s[a].reshape(128, 128) * (1.0 / cells)
        return jnp.concatenate([full[:, :rank], full[:, rank:]], axis=0)

    def tables_of(ref):
        total = jnp.zeros((6 * rank + 16, rank), F32)
        for i in range(no // 512):
            v = ref[:, 512 * i : 512 * i + 512]
            v_hi, v_lo = split(v)
            d = d_ref[:, 512 * i : 512 * i + 512]
            parts = [v * jnp.maximum(sign * d[dim : dim + 1], 0.0) for dim, sign in signs]
            l_hi, l_lo = split(jnp.concatenate(parts + [jnp.ones((16, 512), F32)], axis=0))
            total = total + gram3(l_hi, l_lo, v_hi, v_lo)
        total = total * (1.0 / no)
        return total[: 6 * rank], total[6 * rank : 6 * rank + 1]

    def column(row):
        return jnp.sum(eye * row, axis=1, keepdims=True)

    half_lane = lax.broadcasted_iota(jnp.int32, (3 * rank, 128), 1) < rank

    def doubled(a):
        hi, lo = split(a)
        return jnp.concatenate([hi, lo[:, :rank]], axis=1)

    def pair_left(first, a):
        turned = pltpu.roll(a, rank, 1)
        return jnp.concatenate(
            [doubled(first), doubled(jnp.where(half_lane, a, turned)), doubled(jnp.where(half_lane, turned, a))], axis=0
        )

    def place(j):
        return block(1 + j // 2 + 3 * (j % 2))

    def flux(k, u_col):
        density = jnp.sum(k * u_col, axis=0, keepdims=True)
        return density, speed_of(density) * k

    def prepare(u_col):
        for q in range(slabs):
            density, g = flux(k_s[:, at(q)], u_col)
            den_s[:, at(q)] = density
            g3_s[:, at(q)] = right3(g)

    half = slab // 2
    low, high = slice(0, half), slice(half, slab)

    def prepare_x(i, part, u_col):
        here = slice(nloc + slab * i + part.start, nloc + slab * i + part.stop)
        g3_s[:, here] = right3(flux(khx_s[i, :, part], u_col)[1])

    def prepare_y(u_col):
        for i in range(2):
            at_y = nloc + 2 * slab + 128 * i
            g3_s[:, at_y : at_y + 128] = right3(flux(khy_s[i], u_col)[1])

    def prepare_halo(u_col):
        for i in range(2):
            for part in (low, high):
                prepare_x(i, part, u_col)
        prepare_y(u_col)

    inputs[0].wait()
    st = left3(mm(eye, s_ref[...], NT))
    first_halo = halo_copies(k_s, 0)
    for i, q in enumerate(order):
        inputs[1 + i].wait()
        x_hi, x_lo = split(x_ref[at(q), :])
        k_s[:, at(q)] = bdot(st[:, :rank], x_hi, NT) + bdot(st[:, rank : 2 * rank], x_lo, NT) + bdot(st[:, 2 * rank :], x_hi, NT)
        if i == 1:
            pl.semaphore_wait(barrier, ngx + ngy - 2)
            for n in (4, 5, 0, 1):
                first_halo[n].start()
    faces(k_s, 0)
    first_halo[2].start()
    first_halo[3].start()
    inputs[slabs + 1].wait()
    inputs[slabs + 2].wait()
    tables, u_row = tables_of(v_ref)
    u_col = column(u_row)
    wide = None
    prepare(u_col)
    k_left = None
    v_now = v_ref
    later = None

    for step in range(STEPS):
        last_step = step == STEPS - 1
        if step == 0:
            center = sum(tables[block(i)] for i in range(1, 6)) + tables[block(0)]
            stencil = left3(c * jnp.concatenate([center] + [tables[block(i)] for i in (0, 2, 4, 1, 3, 5)], axis=0))
        else:
            center = wide[:, :128] + wide[:, 128:256] + wide[:, 256:]
            weights = jnp.concatenate([wide[:, 128 * i : 128 * i + 128] for i in range(3)], axis=0)
            stencil = pair_left(c * (center + pltpu.roll(center, rank, 1)), c * weights)
        bx = nloc
        by = nloc + 2 * slab

        def x_terms(i, part):
            here = slice(bx + slab * i + part.start, bx + slab * i + part.stop)
            there = slice(slab * slabs * i + part.start, slab * slabs * i + part.stop)
            (tpx_s, tmx_s)[i][:, there] = bdot(stencil[place(2 * i)], g3_s[:, here])

        def y_terms():
            return (
                bdot(stencil[place(1)], g3_s[:, by : by + 128]),
                bdot(stencil[place(3)], g3_s[:, by + 128 : by + 256]),
            )

        halo = halo_copies(k1_s, step + 1)

        def spread(q):
            k = k_s[:, at(q)]
            if k_left is not None:
                k = bdot(k_left, right3(k))
            out = bdot(stencil, g3_s[:, at(q)])
            base_s[:, at(q)] = (1.0 - t) * k + t * u_col * den_s[:, at(q)] - out[:rank]
            tpx_s[:, at(q + 1)] = out[place(0)]
            t_s[0, :, at(q)] = out[place(1)]
            tmx_s[:, at(q)] = out[place(2)]
            t_s[1, :, at(q)] = out[place(3)]
            t_s[2, :, at(q)] = out[place(4)]
            t_s[3, :, at(q)] = out[place(5)]

        def combine(q, chunks):
            for n in chunks:
                start = slab * q + 128 * n
                here = slice(start, start + 128)
                back, front = t_s[0, :, here], t_s[1, :, here]
                before = roll(t_s[0, :, start - 128 : start], zlen) if n > 0 else roll(tpy, -zlen * q)
                if n < slab // 128 - 1:
                    after = roll(t_s[1, :, start + 128 : start + 256], -zlen)
                else:
                    after = roll(tmy, 128 - zlen - zlen * q)
                k1_s[:, here] = (
                    base_s[:, here]
                    + tpx_s[:, here]
                    + tmx_s[:, start + slab : start + slab + 128]
                    + jnp.where(lane < zlen, before, roll(back, zlen))
                    + jnp.where(lane < 128 - zlen, roll(front, -zlen), after)
                    + from_z_before(t_s[2, :, here])
                    + from_z_after(t_s[3, :, here])
                )

        ends = slabs - 1
        lows, highs = range(half // 128), range(half // 128, slab // 128)
        if step == 0:
            for q in order:
                spread(q)
            for n in (4, 5, 2, 3):
                first_halo[n].wait()
            for i, part in ((0, high), (1, low)):
                khx_s[i, :, part] = xhalo_s[0, i, :, part]
                khy_s[i] = yhalo_s[0, i]
                prepare_x(i, part, u_col)
                x_terms(i, part)
            prepare_y(u_col)
            tpy, tmy = y_terms()
            combine(0, highs)
            halo[0].start()
            combine(ends, lows)
            halo[1].start()
            for n in (0, 1):
                first_halo[n].wait()
            for i, part in ((0, low), (1, high)):
                khx_s[i, :, part] = xhalo_s[0, i, :, part]
                prepare_x(i, part, u_col)
                x_terms(i, part)
        else:
            for i in range(2):
                for part in (low, high):
                    x_terms(i, part)
            tpy, tmy = y_terms()
            spread(0)
            spread(1)
            combine(0, highs)
            halo[0].start()
            for q in range(ends, 1, -1):
                spread(q)
            combine(ends, lows)
            halo[1].start()
        combine(0, lows)
        combine(ends, highs)
        for q in range(1, ends):
            combine(q, range(slab // 128))
        faces(k1_s, step + 1)
        halo[2].start()
        halo[3].start()

        first, second = 2 * step, 2 * step + 1
        raw = jnp.zeros((4 * rank, rank), F32)
        for q in range(slabs):
            k1 = k1_s[:, at(q)]
            h = flux(k1, u_col)[1]
            h_s[:, at(q)] = h
            l_hi, l_lo = split(jnp.concatenate([k1, h - from_z_before(h), from_z_after(h) - h, h], axis=0))
            kk_s[0, :, at(q)], kk_s[1, :, at(q)] = l_hi[:rank], l_lo[:rank]
            hh_s[0, :, at(q)], hh_s[1, :, at(q)] = l_hi[3 * rank :], l_lo[3 * rank :]
            raw = raw + gram3(l_hi, l_lo, l_hi[:rank], l_lo[:rank])
        pack(first, raw)
        start_phase(first, 0)
        if not last_step:
            halo[4].start()
            halo[5].start()
        h_k1 = raw[3 * rank :]
        if later is not None:
            tables = later()

        sums = {name: jnp.zeros((rank, rank), F32) for name in ("x-", "y-", "x+", "y+")}
        for q in range(slabs):
            h = h_s[:, at(q)]
            y_hi, y_lo = split(jnp.concatenate([from_y_before(h), from_y_after(h)], axis=0))
            names, his, los = ["y-", "y+"], [y_hi], [y_lo]
            for name, other in (("x-", q - 1), ("x+", q + 1)):
                if 0 <= other < slabs:
                    names.append(name)
                    his.append(hh_s[0, :, at(other)])
                    los.append(hh_s[1, :, at(other)])
            out = gram3(jnp.concatenate(his, axis=0), jnp.concatenate(los, axis=0), kk_s[0, :, at(q)], kk_s[1, :, at(q)])
            for i, name in enumerate(names):
                sums[name] = sums[name] + out[block(i)]
        y_first, y_last = split(yface_s[step + 1, 0]), split(yface_s[step + 1, 1])
        own_low, own_high = slice(0, half), slice(nloc - half, nloc)
        for copy in halo[:4]:
            copy.wait()
        before, after = xhalo_s[step + 1, 0, :, low], xhalo_s[step + 1, 1, :, high]
        b_hi, b_lo = split(before)
        a_hi, a_lo = split(after)
        hb_hi, hb_lo = split(flux(before, u_col)[1])
        ha_hi, ha_lo = split(flux(after, u_col)[1])

        def side(x, y):
            return jnp.concatenate([x, y], axis=1)

        sums["x-"] = sums["x-"] + gram3(
            side(hb_hi, hh_s[0, :, own_high]), side(hb_lo, hh_s[1, :, own_high]),
            side(kk_s[0, :, own_low], a_hi), side(kk_s[1, :, own_low], a_lo),
        )
        sums["x+"] = sums["x+"] + gram3(
            side(hh_s[0, :, own_low], ha_hi), side(hh_s[1, :, own_low], ha_lo),
            side(b_hi, kk_s[0, :, own_high]), side(b_lo, kk_s[1, :, own_high]),
        )
        for i, (name, edge) in enumerate((("y-", y_first), ("y+", y_last))):
            hi, lo = split(flux(yhalo_s[step + 1, i], u_col)[1])
            sums[name] = sums[name] + gram3(hi, lo, *edge)
        pack(
            second,
            jnp.concatenate([h_k1 - sums["x-"], h_k1 - sums["y-"], sums["x+"] - h_k1, sums["y+"] - h_k1], axis=0),
        )
        start_phase(second, 0)
        for i in range(no // 512):
            here = slice(512 * i, 512 * i + 512)
            v3_s[:, here] = right3(v_now[:, here])
        for phase in range(2):
            for a in (first, second):
                end_phase(a, phase)
                start_phase(a, phase + 1)
        end_phase(first, 2)
        total = unpack(first)
        upper, inverse = finish(advance(begin(total[:rank]), 0, rank // 8))
        none = jnp.zeros((rank, rank), F32)

        def twice(a):
            return jnp.concatenate(
                [jnp.concatenate([a, none], axis=1), jnp.concatenate([none, a], axis=1)], axis=0
            )

        inverse_2, inverse_t = split(twice(inverse)), split(twice(mm(eye, inverse, NT)))
        q_z = mm3(inverse, total[rank : 3 * rank], NT)
        m_z = dot3(split(q_z), inverse_t)
        signed = jnp.concatenate([tables[: 2 * rank], -tables[2 * rank : 4 * rank], tables[block(4)], -tables[block(5)]], axis=0)
        signed = jnp.concatenate([signed, signed], axis=1)
        s_start = (1.0 + t) * upper - t * (jnp.sum(upper * u_row, axis=1, keepdims=True) * u_row)
        s_start = jnp.concatenate([s_start, s_start], axis=1) + c * mm3(q_z, signed[4 * rank :])
        signed = split(c * signed[: 4 * rank])
        left = left_x = left3(inverse)
        if not last_step:
            for q in range(slabs):
                k_s[:, at(q)] = bdot(left, right3(k1_s[:, at(q)]))
        if not last_step:
            halo[4].wait()
            halo[5].wait()
            for i in range(2):
                khx_s[i] = bdot(left, right3(xhalo_s[step + 1, i]))
                khy_s[i] = bdot(left, right3(yhalo_s[step + 1, i]))
        end_phase(second, 2)
        both = split(dot3(inverse_2, split(r3_s[second].reshape(128, 128) * (1.0 / cells)), NT))
        m_all = jnp.concatenate([dot3(both, inverse_t), m_z], axis=0)
        s2 = s_start + dot3([x[:rank] for x in both], [x[: 2 * rank] for x in signed])
        s2 = s2 + dot3([x[rank:] for x in both], [x[2 * rank :] for x in signed])
        s2_2 = jnp.concatenate([jnp.where(half_lane[:rank], s2, 0.0), jnp.where(half_lane[:rank], 0.0, s2)], axis=0)
        ms2 = mm3(m_all, s2_2)
        mean = jnp.sum(s2[:, :rank] * u_row, axis=1, keepdims=True)
        left = pair_left((1.0 - t) * s2, c * ms2)
        gram = jnp.zeros((rank, rank), F32)
        for i in range(no // 512):
            here = slice(512 * i, 512 * i + 512)
            out = bdot(left, v3_s[:, here])
            d = d_ref[:, here]
            l1 = out[:rank] + t * mean
            for j, (dim, sign) in enumerate(signs):
                l1 = l1 - (sign * jnp.maximum(sign * d[dim : dim + 1], 0.0)) * out[place(j)]
            v_s[:, here] = l1
            hi, lo = split(l1)
            gram = gram + gram3(hi, lo, hi, lo)
        v_now = v_s
        v_upper, v_inverse = finish(advance(begin(gram * (1.0 / no)), 0, rank // 8))
        if last_step:
            for q in range(slabs):
                x1 = bdot(left_x, right3(k1_s[:, at(q)]))
                x_out[at(q), :] = jnp.concatenate([x1, x1], axis=0).T[:, :rank]
            left = left3(v_inverse)
            for i in range(no // 512):
                here = slice(512 * i, 512 * i + 512)
                v_out[:, here] = bdot(left, right3(v_s[:, here]))
            s_out[...] = mm(eye, v_upper, NT)
        else:
            raw_tables, raw_row = tables_of(v_s)
            table_parts = split(raw_tables)
            raw_col = column(raw_row)
            prepare(raw_col)
            prepare_halo(raw_col)
            left = left3(v_inverse)
            wide = dot3(split(v_inverse), table_parts, NT)
            u_col = jnp.sum(v_inverse * raw_row, axis=1, keepdims=True)
            u_row = jnp.sum(eye * u_col, axis=0, keepdims=True)
            k_left = left3(v_upper)

            def later(left=left, wide=wide, v_inverse=v_inverse):
                for i in range(no // 512):
                    here = slice(512 * i, 512 * i + 512)
                    v_s[:, here] = bdot(left, right3(v_s[:, here]))
                return mm(jnp.concatenate([wide[:, block(i)] for i in range(6)], axis=0), v_inverse, NT)

    def drain(a, _):
        for phase in range(3):
            all_of(a, phase, asend).wait()
        return 0

    lax.fori_loop(0, 2 * STEPS, drain, 0)


def store(x_ref, s_ref, v_ref, x_out, s_out, v_out, sems):
    copies = [
        pltpu.make_async_copy(src, dst, sems.at[i])
        for i, (src, dst) in enumerate(((x_ref, x_out), (v_ref, v_out), (s_ref, s_out)))
    ]
    for copy in copies:
        copy.start()
    for copy in copies:
        copy.wait()


def solution(mesh):
    ngx, ngy = mesh.shape["gx"], mesh.shape["gy"]

    def shards(spatial, coupling, orient, directions):
        slabs, ylen, zlen, rank = spatial.shape
        slab = ylen * zlen
        nloc = slabs * slab
        no = orient.shape[0]
        crow = 128 // ngy
        vmem, hbm = pl.BlockSpec(memory_space=pltpu.VMEM), pl.BlockSpec(memory_space=pltpu.HBM)
        sums = 2 * STEPS
        scratch = [
            (nloc, rank), (rank, rank), (rank, no), (3, no),
            (rank, nloc), (rank, nloc), (rank, nloc + slab), (rank, nloc + slab), (4, rank, nloc), (rank, nloc),
            (rank, nloc), (2, rank, slab), (2, rank, 128), (rank, no),
            (STEPS + 1, 2, rank, 128), (STEPS + 1, 2, rank, slab), (STEPS + 1, 2, rank, 128),
            (sums, ngy, crow, 128), (sums, ngy, crow, 128), (sums, crow, 128), (sums, ngx, crow, 128),
            (sums, crow, 128), (sums, ngy, crow, 128), (1, nloc),
        ]
        outs = (
            jax.ShapeDtypeStruct((nloc, rank), F32),
            jax.ShapeDtypeStruct((rank, rank), F32),
            jax.ShapeDtypeStruct((rank, no), F32),
        )
        results = pl.pallas_call(
            functools.partial(kernel, (ngx, ngy, slabs, ylen, zlen)),
            out_shape=outs,
            in_specs=[hbm] * 4,
            out_specs=(vmem, vmem, vmem),
            scratch_shapes=[pltpu.VMEM(shape, F32) for shape in scratch]
            + [
                pltpu.VMEM((3 * rank, nloc + 2 * slab + 256), BF16),
                pltpu.VMEM((2, rank, nloc), BF16),
                pltpu.VMEM((2, rank, nloc), BF16),
                pltpu.VMEM((3 * rank, no), BF16),
                pltpu.SemaphoreType.DMA((slabs + 3,)),
                pltpu.SemaphoreType.DMA((STEPS + 1, 6)),
                pltpu.SemaphoreType.DMA((STEPS + 1, 6)),
                pltpu.SemaphoreType.DMA((sums, 3)),
                pltpu.SemaphoreType.DMA((sums, 3)),
            ],
            compiler_params=pltpu.CompilerParams(
                collective_id=0, has_side_effects=True, vmem_limit_bytes=40 * 1024 * 1024
            ),
        )(*[pltpu.with_memory_space_constraint(a, pltpu.HBM) for a in (spatial.reshape(nloc, rank), coupling, orient.T, directions)])
        x, s, v = pl.pallas_call(
            store,
            out_shape=outs,
            in_specs=[vmem] * 3,
            out_specs=(hbm, hbm, hbm),
            scratch_shapes=[pltpu.SemaphoreType.DMA((3,))],
            compiler_params=pltpu.CompilerParams(vmem_limit_bytes=1024 * 1024),
        )(*results)
        return x.reshape(spatial.shape), s, v.T

    return jax.shard_map(
        shards,
        mesh=mesh,
        in_specs=(P("gx", "gy", None, None), P(), P(), P()),
        out_specs=(P("gx", "gy", None, None), P(), P()),
        check_vma=False,
    )
```

```python
import functools

import jax
import jax.numpy as jnp
from jax import lax
from jax.experimental import pallas as pl
from jax.experimental.pallas import tpu as pltpu
from jax.sharding import PartitionSpec as P

STEPS = 2
MESH = pl.DeviceIdType.MESH
F32 = jnp.float32
BF16 = jnp.bfloat16
NN = (((1,), (0,)), ((), ()))
NT = (((1,), (1,)), ((), ()))

courant = 0.3
tumble = 0.2


def mm(a, b, dims=NN):
    return lax.dot_general(a, b, dims, precision=lax.Precision.HIGHEST, preferred_element_type=F32)


def bdot(a, b, dims=NN):
    return lax.dot_general(a, b, dims, preferred_element_type=F32)


def split(a):
    hi = a.astype(BF16)
    return hi, (a - hi.astype(F32)).astype(BF16)


def left3(a):
    hi, lo = split(a)
    return jnp.concatenate([hi, hi, lo], axis=1)


def right3(b):
    hi, lo = split(b)
    return jnp.concatenate([hi, lo, hi], axis=0)


def dot3(a, b, dims=NN):
    return bdot(a[0], b[0], dims) + (bdot(a[0], b[1], dims) + bdot(a[1], b[0], dims))


def mm3(a, b, dims=NN):
    return dot3(split(a), split(b), dims)


def gram3(left_hi, left_lo, right_hi, right_lo):
    width = right_hi.shape[0]
    first = bdot(left_hi, jnp.concatenate([right_hi, right_lo], axis=0), NT)
    return first[:, :width] + first[:, width:] + bdot(left_lo, right_hi, NT)


def speed_of(density):
    return 1.0 / (1.0 + density * density)


def begin(gram):
    n = gram.shape[0]
    eye = jnp.where(lax.broadcasted_iota(jnp.int32, (n, n), 0) == lax.broadcasted_iota(jnp.int32, (n, n), 1), 1.0, 0.0)
    both = jnp.concatenate([gram, eye], axis=1)
    return [both[8 * b : 8 * b + 8] for b in range(n // 8)]


def advance(blocks, start, stop):
    width = blocks[0].shape[1]
    below = lax.broadcasted_iota(jnp.int32, (8, width), 0)

    def across(a, c):
        return jnp.broadcast_to(a[:, c : c + 1], (8, width))

    def down(a, r):
        return jnp.broadcast_to(a[r : r + 1], (8, width))

    count = len(blocks)
    own = [across(blocks[start], 8 * start + c) for c in range(8)]
    for kb in range(start, stop):
        under = {n: [across(blocks[n], 8 * kb + c) for c in range(8)] for n in range(kb + 1, count)}
        ahead = [across(blocks[kb + 1], 8 * kb + 8 + c) for c in range(8)] if kb + 1 < count else None
        current = blocks[kb]
        a, b, d = down(own[0], 0), down(own[1], 0), down(own[1], 1)
        for k in range(0, 8, 2):
            first = {j: down(own[j], k) for j in range(k + 2, 8)}
            second = {j: down(own[j], k + 1) for j in range(k + 2, 8)}
            inverse = 1.0 / (a * d - b * b)
            p, q, r = d * inverse, b * inverse, a * inverse
            ratio = b / a
            if k < 6:
                x0, x1, y0, y1 = down(own[k], k + 2), down(own[k + 1], k + 2), down(own[k], k + 3), down(own[k + 1], k + 3)
                xd, yd = x0 * d - x1 * b, y0 * d - y1 * b
                xa, ya = x1 * a - x0 * b, y1 * a - y0 * b
                a, b, d = (
                    down(own[k + 2], k + 2) - (x0 * xd + x1 * xa) * inverse,
                    down(own[k + 3], k + 2) - (x0 * yd + x1 * ya) * inverse,
                    down(own[k + 3], k + 3) - (y0 * yd + y1 * ya) * inverse,
                )
            rows = down(current, k), down(current, k + 1)
            f1 = jnp.where(below > k + 1, own[k] * p - own[k + 1] * q, 0.0)
            f2 = jnp.where(below > k + 1, own[k + 1] * r - own[k] * q, 0.0)
            for j in range(k + 2, 8):
                own[j] = own[j] - f1 * first[j] - f2 * second[j]
            f1 = jnp.where(below == k + 1, ratio, f1)
            current = current - f1 * rows[0] - f2 * rows[1]
            for n, columns in under.items():
                f1 = columns[k] * p - columns[k + 1] * q
                f2 = columns[k + 1] * r - columns[k] * q
                for j in range(k + 2, 8):
                    columns[j] = columns[j] - f1 * first[j] - f2 * second[j]
                if n == kb + 1:
                    for c in range(8):
                        ahead[c] = ahead[c] - f1 * down(columns[k], c) - f2 * down(columns[k + 1], c)
                blocks[n] = blocks[n] - f1 * rows[0] - f2 * rows[1]
        blocks[kb] = current
        own = ahead
    return blocks


def finish(blocks):
    whole = jnp.concatenate(blocks, axis=0)
    n = whole.shape[0]
    i, j = (lax.broadcasted_iota(jnp.int32, (n, n), d) for d in range(2))
    diagonal = jnp.sum(jnp.where(i == j, whole[:, :n], 0.0), axis=1, keepdims=True)
    whole = whole * (1.0 / jnp.sqrt(diagonal))
    return jnp.where(j >= i, whole[:, :n], 0.0), whole[:, n:]


def kernel(
    sizes, x_hbm, s_hbm, v_hbm, d_hbm, x_out, s_out, v_out, x_ref, s_ref, v_ref, d_ref,
    k_s, base_s, tpx_s, tmx_s, t_s, k1_s, h_s, khx_s, khy_s, v_s, yface_s,
    xhalo_s, yhalo_s, pay_s, r1_s, c_s, r2_s, f_s, r3_s, den_s, g3_s, kk_s, hh_s, v3_s,
    isem, hsend, hrecv, asend, arecv,
):
    ngx, ngy, slabs, ylen, zlen = sizes
    slab = ylen * zlen
    nloc = slabs * slab
    cells = float(nloc * ngx * ngy)
    no = v_hbm.shape[1]
    rank = 64
    c, t = courant, tumble
    me_x, me_y = lax.axis_index("gx"), lax.axis_index("gy")
    crow = 128 // ngy
    signs = ((0, 1), (1, 1), (0, -1), (1, -1), (2, 1), (2, -1))

    order = (0, slabs - 1) + tuple(range(1, slabs - 1))
    inputs = [pltpu.make_async_copy(s_hbm, s_ref, isem.at[0])]
    for q in order:
        rows = pl.ds(slab * q, slab)
        inputs.append(pltpu.make_async_copy(x_hbm.at[rows], x_ref.at[rows], isem.at[1 + q]))
    inputs.append(pltpu.make_async_copy(v_hbm, v_ref, isem.at[slabs + 1]))
    inputs.append(pltpu.make_async_copy(d_hbm, d_ref, isem.at[slabs + 2]))
    for copy in inputs:
        copy.start()

    barrier = pltpu.get_barrier_semaphore()

    def greet_x(i, _):
        pl.semaphore_signal(barrier, inc=1, device_id={"gx": lax.rem(me_x + i, ngx), "gy": me_y}, device_id_type=MESH)
        return 0

    def greet_y(i, _):
        pl.semaphore_signal(barrier, inc=1, device_id={"gx": me_x, "gy": lax.rem(me_y + i, ngy)}, device_id_type=MESH)
        return 0

    lax.fori_loop(1, ngx, greet_x, 0)
    lax.fori_loop(1, ngy, greet_y, 0)

    eye = jnp.where(
        lax.broadcasted_iota(jnp.int32, (rank, rank), 0) == lax.broadcasted_iota(jnp.int32, (rank, rank), 1), 1.0, 0.0
    )
    lane = lax.broadcasted_iota(jnp.int32, (rank, 128), 1)
    zpos = lax.rem(lane, zlen)
    group = lane // zlen

    def at(q):
        return slice(slab * q, slab * q + slab)

    def block(i):
        return slice(rank * i, rank * i + rank)

    def cut(a):
        return [a[:, 128 * i : 128 * i + 128] for i in range(a.shape[1] // 128)]

    def roll(a, s):
        s = s % 128
        return a if s == 0 else pltpu.roll(a, s, 1)

    def from_y_before(a, halo=None, q=0):
        last = 0.0 if halo is None else roll(halo, zlen * (-q))
        out = []
        for piece in [roll(piece, zlen) for piece in cut(a)]:
            out.append(jnp.where(lane < zlen, last, piece))
            last = piece
        return jnp.concatenate(out, axis=1)

    def from_y_after(a, halo=None, q=0):
        rolled = [roll(piece, -zlen) for piece in cut(a)]
        rolled.append(0.0 if halo is None else roll(halo, 128 - zlen - zlen * q))
        return jnp.concatenate(
            [jnp.where(lane < 128 - zlen, rolled[i], rolled[i + 1]) for i in range(len(rolled) - 1)], axis=1
        )

    def from_z_before(a):
        return jnp.concatenate([jnp.where(zpos == 0, roll(p, 1 - zlen), roll(p, 1)) for p in cut(a)], axis=1)

    def from_z_after(a):
        return jnp.concatenate([jnp.where(zpos == zlen - 1, roll(p, zlen - 1), roll(p, -1)) for p in cut(a)], axis=1)

    def faces(ref, e):
        first, last = jnp.zeros((rank, 128), F32), jnp.zeros((rank, 128), F32)
        for q in range(slabs):
            low = ref[:, slab * q : slab * q + 128]
            high = ref[:, slab * q + slab - 128 : slab * q + slab]
            first = jnp.where(group == q, roll(low, zlen * q), first)
            last = jnp.where(group == q, roll(high, zlen * q - (128 - zlen)), last)
        yface_s[e, 0] = first
        yface_s[e, 1] = last

    def halo_copies(ref, e):
        left = {"gx": lax.rem(me_x + ngx - 1, ngx), "gy": me_y}
        right = {"gx": lax.rem(me_x + 1, ngx), "gy": me_y}
        under = {"gx": me_x, "gy": lax.rem(me_y + ngy - 1, ngy)}
        over = {"gx": me_x, "gy": lax.rem(me_y + 1, ngy)}
        half = slab // 2
        low, high = pl.ds(0, half), pl.ds(half, half)
        end = nloc - slab
        plan = [
            (ref.at[:, pl.ds(half, half)], xhalo_s.at[e, 1, :, high], left),
            (ref.at[:, pl.ds(end, half)], xhalo_s.at[e, 0, :, low], right),
            (yface_s.at[e, 1], yhalo_s.at[e, 0], over),
            (yface_s.at[e, 0], yhalo_s.at[e, 1], under),
            (ref.at[:, pl.ds(0, half)], xhalo_s.at[e, 1, :, low], left),
            (ref.at[:, pl.ds(end + half, half)], xhalo_s.at[e, 0, :, high], right),
        ]
        return [
            pltpu.make_async_remote_copy(
                src_ref=src, dst_ref=dst, send_sem=hsend.at[e, i], recv_sem=hrecv.at[e, i], device_id=to, device_id_type=MESH
            )
            for i, (src, dst, to) in enumerate(plan)
        ]

    landing = (r1_s, r2_s, r3_s)

    def start_phase(a, phase):
        mine, n = (me_x, ngx) if phase == 1 else (me_y, ngy)
        for i in sorted(range(1, n), key=lambda i: -min(i, n - i)):
            other = lax.rem(mine + i, n)
            pltpu.make_async_remote_copy(
                src_ref=pay_s.at[a, other] if phase == 0 else (c_s if phase == 1 else f_s).at[a],
                dst_ref=landing[phase].at[a, mine],
                send_sem=asend.at[a, phase],
                recv_sem=arecv.at[a, phase],
                device_id={"gx": other, "gy": me_y} if phase == 1 else {"gx": me_x, "gy": other},
                device_id_type=MESH,
            ).start()
        if phase == 0:
            r1_s[a, me_y] = pay_s[a, me_y]
        elif phase == 1:
            r2_s[a, me_x] = c_s[a]
        else:
            r3_s[a, me_y] = f_s[a]

    def all_of(a, phase, sem):
        part = landing[phase].at[a, pl.ds(0, (ngx if phase == 1 else ngy) - 1)]
        return pltpu.make_async_copy(part, part, sem.at[a, phase])

    def end_phase(a, phase):
        all_of(a, phase, arecv).wait()
        if phase == 0:
            c_s[a] = jnp.sum(r1_s[a], axis=0)
        elif phase == 1:
            f_s[a] = jnp.sum(r2_s[a], axis=0)

    def pack(a, raw):
        pay_s[a] = jnp.concatenate([raw[: 2 * rank], raw[2 * rank :]], axis=1).reshape(ngy, crow, 128)

    def unpack(a):
        full = r3_s[a].reshape(128, 128) * (1.0 / cells)
        return jnp.concatenate([full[:, :rank], full[:, rank:]], axis=0)

    def tables_of(ref):
        total = jnp.zeros((6 * rank + 16, rank), F32)
        for i in range(no // 512):
            v = ref[:, 512 * i : 512 * i + 512]
            v_hi, v_lo = split(v)
            d = d_ref[:, 512 * i : 512 * i + 512]
            parts = [v * jnp.maximum(sign * d[dim : dim + 1], 0.0) for dim, sign in signs]
            l_hi, l_lo = split(jnp.concatenate(parts + [jnp.ones((16, 512), F32)], axis=0))
            total = total + gram3(l_hi, l_lo, v_hi, v_lo)
        total = total * (1.0 / no)
        return total[: 6 * rank], total[6 * rank : 6 * rank + 1]

    def column(row):
        return jnp.sum(eye * row, axis=1, keepdims=True)

    half_lane = lax.broadcasted_iota(jnp.int32, (3 * rank, 128), 1) < rank

    def doubled(a):
        hi, lo = split(a)
        return jnp.concatenate([hi, lo[:, :rank]], axis=1)

    def pair_left(first, a):
        turned = pltpu.roll(a, rank, 1)
        return jnp.concatenate(
            [doubled(first), doubled(jnp.where(half_lane, a, turned)), doubled(jnp.where(half_lane, turned, a))], axis=0
        )

    def place(j):
        return block(1 + j // 2 + 3 * (j % 2))

    def flux(k, u_col):
        density = jnp.sum(k * u_col, axis=0, keepdims=True)
        return density, speed_of(density) * k

    def prepare(u_col):
        for q in range(slabs):
            density, g = flux(k_s[:, at(q)], u_col)
            den_s[:, at(q)] = density
            g3_s[:, at(q)] = right3(g)

    half = slab // 2
    low, high = slice(0, half), slice(half, slab)

    def prepare_x(i, part, u_col):
        here = slice(nloc + slab * i + part.start, nloc + slab * i + part.stop)
        g3_s[:, here] = right3(flux(khx_s[i, :, part], u_col)[1])

    def prepare_y(u_col):
        for i in range(2):
            at_y = nloc + 2 * slab + 128 * i
            g3_s[:, at_y : at_y + 128] = right3(flux(khy_s[i], u_col)[1])

    def prepare_halo(u_col):
        for i in range(2):
            for part in (low, high):
                prepare_x(i, part, u_col)
        prepare_y(u_col)

    inputs[0].wait()
    st = left3(mm(eye, s_ref[...], NT))
    first_halo = halo_copies(k_s, 0)
    for i, q in enumerate(order):
        inputs[1 + i].wait()
        x_hi, x_lo = split(x_ref[at(q), :])
        k_s[:, at(q)] = bdot(st[:, :rank], x_hi, NT) + bdot(st[:, rank : 2 * rank], x_lo, NT) + bdot(st[:, 2 * rank :], x_hi, NT)
        if i == 1:
            pl.semaphore_wait(barrier, ngx + ngy - 2)
            for n in (4, 5, 0, 1):
                first_halo[n].start()
    faces(k_s, 0)
    first_halo[2].start()
    first_halo[3].start()
    inputs[slabs + 1].wait()
    inputs[slabs + 2].wait()
    tables, u_row = tables_of(v_ref)
    u_col = column(u_row)
    wide = None
    prepare(u_col)
    k_left = None
    v_now = v_ref
    later = None

    for step in range(STEPS):
        last_step = step == STEPS - 1
        if step == 0:
            center = sum(tables[block(i)] for i in range(1, 6)) + tables[block(0)]
            stencil = left3(c * jnp.concatenate([center] + [tables[block(i)] for i in (0, 2, 4, 1, 3, 5)], axis=0))
        else:
            center = wide[:, :128] + wide[:, 128:256] + wide[:, 256:]
            weights = jnp.concatenate([wide[:, 128 * i : 128 * i + 128] for i in range(3)], axis=0)
            stencil = pair_left(c * (center + pltpu.roll(center, rank, 1)), c * weights)
        bx = nloc
        by = nloc + 2 * slab

        def x_terms(i, part):
            here = slice(bx + slab * i + part.start, bx + slab * i + part.stop)
            there = slice(slab * slabs * i + part.start, slab * slabs * i + part.stop)
            (tpx_s, tmx_s)[i][:, there] = bdot(stencil[place(2 * i)], g3_s[:, here])

        def y_terms():
            return (
                bdot(stencil[place(1)], g3_s[:, by : by + 128]),
                bdot(stencil[place(3)], g3_s[:, by + 128 : by + 256]),
            )

        halo = halo_copies(k1_s, step + 1)

        def spread(q):
            k = k_s[:, at(q)]
            if k_left is not None:
                k = bdot(k_left, right3(k))
            out = bdot(stencil, g3_s[:, at(q)])
            base_s[:, at(q)] = (1.0 - t) * k + t * u_col * den_s[:, at(q)] - out[:rank]
            tpx_s[:, at(q + 1)] = out[place(0)]
            t_s[0, :, at(q)] = out[place(1)]
            tmx_s[:, at(q)] = out[place(2)]
            t_s[1, :, at(q)] = out[place(3)]
            t_s[2, :, at(q)] = out[place(4)]
            t_s[3, :, at(q)] = out[place(5)]

        def combine(q, chunks):
            for n in chunks:
                start = slab * q + 128 * n
                here = slice(start, start + 128)
                back, front = t_s[0, :, here], t_s[1, :, here]
                before = roll(t_s[0, :, start - 128 : start], zlen) if n > 0 else roll(tpy, -zlen * q)
                if n < slab // 128 - 1:
                    after = roll(t_s[1, :, start + 128 : start + 256], -zlen)
                else:
                    after = roll(tmy, 128 - zlen - zlen * q)
                k1_s[:, here] = (
                    base_s[:, here]
                    + tpx_s[:, here]
                    + tmx_s[:, start + slab : start + slab + 128]
                    + jnp.where(lane < zlen, before, roll(back, zlen))
                    + jnp.where(lane < 128 - zlen, roll(front, -zlen), after)
                    + from_z_before(t_s[2, :, here])
                    + from_z_after(t_s[3, :, here])
                )

        ends = slabs - 1
        lows, highs = range(half // 128), range(half // 128, slab // 128)
        if step == 0:
            for q in order:
                spread(q)
            for n in (4, 5, 2, 3):
                first_halo[n].wait()
            for i, part in ((0, high), (1, low)):
                khx_s[i, :, part] = xhalo_s[0, i, :, part]
                khy_s[i] = yhalo_s[0, i]
                prepare_x(i, part, u_col)
                x_terms(i, part)
            prepare_y(u_col)
            tpy, tmy = y_terms()
            combine(0, highs)
            halo[0].start()
            combine(ends, lows)
            halo[1].start()
            for n in (0, 1):
                first_halo[n].wait()
            for i, part in ((0, low), (1, high)):
                khx_s[i, :, part] = xhalo_s[0, i, :, part]
                prepare_x(i, part, u_col)
                x_terms(i, part)
        else:
            for i in range(2):
                for part in (low, high):
                    x_terms(i, part)
            tpy, tmy = y_terms()
            spread(0)
            spread(1)
            combine(0, highs)
            halo[0].start()
            for q in range(ends, 1, -1):
                spread(q)
            combine(ends, lows)
            halo[1].start()
        tail = slab // 128 - 1
        combine(0, (0,))
        combine(ends, (tail,))
        for q in range(1, ends):
            combine(q, (0, tail))
        faces(k1_s, step + 1)
        halo[2].start()
        halo[3].start()
        combine(0, lows[1:])
        combine(ends, highs[:-1])
        for q in range(1, ends):
            combine(q, range(1, tail))

        first, second = 2 * step, 2 * step + 1
        raw = jnp.zeros((4 * rank, rank), F32)
        for q in range(slabs):
            k1 = k1_s[:, at(q)]
            h = flux(k1, u_col)[1]
            h_s[:, at(q)] = h
            l_hi, l_lo = split(jnp.concatenate([k1, h - from_z_before(h), from_z_after(h) - h, h], axis=0))
            kk_s[0, :, at(q)], kk_s[1, :, at(q)] = l_hi[:rank], l_lo[:rank]
            hh_s[0, :, at(q)], hh_s[1, :, at(q)] = l_hi[3 * rank :], l_lo[3 * rank :]
            raw = raw + gram3(l_hi, l_lo, l_hi[:rank], l_lo[:rank])
        pack(first, raw)
        start_phase(first, 0)
        h_k1 = raw[3 * rank :]
        if later is not None:
            tables = later()

        sums = {name: jnp.zeros((rank, rank), F32) for name in ("x-", "y-", "x+", "y+")}
        for q in range(slabs):
            h = h_s[:, at(q)]
            y_hi, y_lo = split(jnp.concatenate([from_y_before(h), from_y_after(h)], axis=0))
            names, his, los = ["y-", "y+"], [y_hi], [y_lo]
            for name, other in (("x-", q - 1), ("x+", q + 1)):
                if 0 <= other < slabs:
                    names.append(name)
                    his.append(hh_s[0, :, at(other)])
                    los.append(hh_s[1, :, at(other)])
            out = gram3(jnp.concatenate(his, axis=0), jnp.concatenate(los, axis=0), kk_s[0, :, at(q)], kk_s[1, :, at(q)])
            for i, name in enumerate(names):
                sums[name] = sums[name] + out[block(i)]
        y_first, y_last = split(yface_s[step + 1, 0]), split(yface_s[step + 1, 1])
        own_low, own_high = slice(0, half), slice(nloc - half, nloc)
        for copy in halo[:4]:
            copy.wait()
        before, after = xhalo_s[step + 1, 0, :, low], xhalo_s[step + 1, 1, :, high]
        b_hi, b_lo = split(before)
        a_hi, a_lo = split(after)
        hb_hi, hb_lo = split(flux(before, u_col)[1])
        ha_hi, ha_lo = split(flux(after, u_col)[1])

        def side(x, y):
            return jnp.concatenate([x, y], axis=1)

        sums["x-"] = sums["x-"] + gram3(
            side(hb_hi, hh_s[0, :, own_high]), side(hb_lo, hh_s[1, :, own_high]),
            side(kk_s[0, :, own_low], a_hi), side(kk_s[1, :, own_low], a_lo),
        )
        sums["x+"] = sums["x+"] + gram3(
            side(hh_s[0, :, own_low], ha_hi), side(hh_s[1, :, own_low], ha_lo),
            side(b_hi, kk_s[0, :, own_high]), side(b_lo, kk_s[1, :, own_high]),
        )
        for i, (name, edge) in enumerate((("y-", y_first), ("y+", y_last))):
            hi, lo = split(flux(yhalo_s[step + 1, i], u_col)[1])
            sums[name] = sums[name] + gram3(hi, lo, *edge)
        pack(
            second,
            jnp.concatenate([h_k1 - sums["x-"], h_k1 - sums["y-"], sums["x+"] - h_k1, sums["y+"] - h_k1], axis=0),
        )
        start_phase(second, 0)
        if not last_step:
            halo[4].start()
            halo[5].start()
        for i in range(no // 512):
            here = slice(512 * i, 512 * i + 512)
            v3_s[:, here] = right3(v_now[:, here])
        for phase in range(2):
            for a in (first, second):
                end_phase(a, phase)
                start_phase(a, phase + 1)
        end_phase(first, 2)
        total = unpack(first)
        upper, inverse = finish(advance(begin(total[:rank]), 0, rank // 8))
        none = jnp.zeros((rank, rank), F32)

        def twice(a):
            return jnp.concatenate(
                [jnp.concatenate([a, none], axis=1), jnp.concatenate([none, a], axis=1)], axis=0
            )

        inverse_2, inverse_t = split(twice(inverse)), split(twice(mm(eye, inverse, NT)))
        q_z = mm3(inverse, total[rank : 3 * rank], NT)
        m_z = dot3(split(q_z), inverse_t)
        signed = jnp.concatenate([tables[: 2 * rank], -tables[2 * rank : 4 * rank], tables[block(4)], -tables[block(5)]], axis=0)
        signed = jnp.concatenate([signed, signed], axis=1)
        s_start = (1.0 + t) * upper - t * (jnp.sum(upper * u_row, axis=1, keepdims=True) * u_row)
        s_start = jnp.concatenate([s_start, s_start], axis=1) + c * mm3(q_z, signed[4 * rank :])
        signed = split(c * signed[: 4 * rank])
        left = left_x = left3(inverse)
        if not last_step:
            for q in range(slabs):
                k_s[:, at(q)] = bdot(left, right3(k1_s[:, at(q)]))
        if not last_step:
            halo[4].wait()
            halo[5].wait()
            for i in range(2):
                khx_s[i] = bdot(left, right3(xhalo_s[step + 1, i]))
                khy_s[i] = bdot(left, right3(yhalo_s[step + 1, i]))
        end_phase(second, 2)
        both = split(dot3(inverse_2, split(r3_s[second].reshape(128, 128) * (1.0 / cells)), NT))
        m_all = jnp.concatenate([dot3(both, inverse_t), m_z], axis=0)
        s2 = s_start + dot3([x[:rank] for x in both], [x[: 2 * rank] for x in signed])
        s2 = s2 + dot3([x[rank:] for x in both], [x[2 * rank :] for x in signed])
        s2_2 = jnp.concatenate([jnp.where(half_lane[:rank], s2, 0.0), jnp.where(half_lane[:rank], 0.0, s2)], axis=0)
        ms2 = mm3(m_all, s2_2)
        mean = jnp.sum(s2[:, :rank] * u_row, axis=1, keepdims=True)
        left = pair_left((1.0 - t) * s2, c * ms2)
        gram = jnp.zeros((rank, rank), F32)
        for i in range(no // 512):
            here = slice(512 * i, 512 * i + 512)
            out = bdot(left, v3_s[:, here])
            d = d_ref[:, here]
            l1 = out[:rank] + t * mean
            for j, (dim, sign) in enumerate(signs):
                l1 = l1 - (sign * jnp.maximum(sign * d[dim : dim + 1], 0.0)) * out[place(j)]
            v_s[:, here] = l1
            hi, lo = split(l1)
            gram = gram + gram3(hi, lo, hi, lo)
        v_now = v_s
        v_upper, v_inverse = finish(advance(begin(gram * (1.0 / no)), 0, rank // 8))
        if last_step:
            for q in range(slabs):
                x1 = bdot(left_x, right3(k1_s[:, at(q)]))
                x_out[at(q), :] = jnp.concatenate([x1, x1], axis=0).T[:, :rank]
            left = left3(v_inverse)
            for i in range(no // 512):
                here = slice(512 * i, 512 * i + 512)
                v_out[:, here] = bdot(left, right3(v_s[:, here]))
            s_out[...] = mm(eye, v_upper, NT)
        else:
            raw_tables, raw_row = tables_of(v_s)
            table_parts = split(raw_tables)
            raw_col = column(raw_row)
            prepare(raw_col)
            prepare_halo(raw_col)
            left = left3(v_inverse)
            wide = dot3(split(v_inverse), table_parts, NT)
            u_col = jnp.sum(v_inverse * raw_row, axis=1, keepdims=True)
            u_row = jnp.sum(eye * u_col, axis=0, keepdims=True)
            k_left = left3(v_upper)

            def later(left=left, wide=wide, v_inverse=v_inverse):
                for i in range(no // 512):
                    here = slice(512 * i, 512 * i + 512)
                    v_s[:, here] = bdot(left, right3(v_s[:, here]))
                return mm(jnp.concatenate([wide[:, block(i)] for i in range(6)], axis=0), v_inverse, NT)

    def drain(a, _):
        for phase in range(3):
            all_of(a, phase, asend).wait()
        return 0

    lax.fori_loop(0, 2 * STEPS, drain, 0)


def store(x_ref, s_ref, v_ref, x_out, s_out, v_out, sems):
    copies = [
        pltpu.make_async_copy(src, dst, sems.at[i])
        for i, (src, dst) in enumerate(((x_ref, x_out), (v_ref, v_out), (s_ref, s_out)))
    ]
    for copy in copies:
        copy.start()
    for copy in copies:
        copy.wait()


def solution(mesh):
    ngx, ngy = mesh.shape["gx"], mesh.shape["gy"]

    def shards(spatial, coupling, orient, directions):
        slabs, ylen, zlen, rank = spatial.shape
        slab = ylen * zlen
        nloc = slabs * slab
        no = orient.shape[0]
        crow = 128 // ngy
        vmem, hbm = pl.BlockSpec(memory_space=pltpu.VMEM), pl.BlockSpec(memory_space=pltpu.HBM)
        sums = 2 * STEPS
        scratch = [
            (nloc, rank), (rank, rank), (rank, no), (3, no),
            (rank, nloc), (rank, nloc), (rank, nloc + slab), (rank, nloc + slab), (4, rank, nloc), (rank, nloc),
            (rank, nloc), (2, rank, slab), (2, rank, 128), (rank, no),
            (STEPS + 1, 2, rank, 128), (STEPS + 1, 2, rank, slab), (STEPS + 1, 2, rank, 128),
            (sums, ngy, crow, 128), (sums, ngy, crow, 128), (sums, crow, 128), (sums, ngx, crow, 128),
            (sums, crow, 128), (sums, ngy, crow, 128), (1, nloc),
        ]
        outs = (
            jax.ShapeDtypeStruct((nloc, rank), F32),
            jax.ShapeDtypeStruct((rank, rank), F32),
            jax.ShapeDtypeStruct((rank, no), F32),
        )
        results = pl.pallas_call(
            functools.partial(kernel, (ngx, ngy, slabs, ylen, zlen)),
            out_shape=outs,
            in_specs=[hbm] * 4,
            out_specs=(vmem, vmem, vmem),
            scratch_shapes=[pltpu.VMEM(shape, F32) for shape in scratch]
            + [
                pltpu.VMEM((3 * rank, nloc + 2 * slab + 256), BF16),
                pltpu.VMEM((2, rank, nloc), BF16),
                pltpu.VMEM((2, rank, nloc), BF16),
                pltpu.VMEM((3 * rank, no), BF16),
                pltpu.SemaphoreType.DMA((slabs + 3,)),
                pltpu.SemaphoreType.DMA((STEPS + 1, 6)),
                pltpu.SemaphoreType.DMA((STEPS + 1, 6)),
                pltpu.SemaphoreType.DMA((sums, 3)),
                pltpu.SemaphoreType.DMA((sums, 3)),
            ],
            compiler_params=pltpu.CompilerParams(
                collective_id=0, has_side_effects=True, vmem_limit_bytes=40 * 1024 * 1024
            ),
        )(*[pltpu.with_memory_space_constraint(a, pltpu.HBM) for a in (spatial.reshape(nloc, rank), coupling, orient.T, directions)])
        x, s, v = pl.pallas_call(
            store,
            out_shape=outs,
            in_specs=[vmem] * 3,
            out_specs=(hbm, hbm, hbm),
            scratch_shapes=[pltpu.SemaphoreType.DMA((3,))],
            compiler_params=pltpu.CompilerParams(vmem_limit_bytes=1024 * 1024),
        )(*results)
        return x.reshape(spatial.shape), s, v.T

    return jax.shard_map(
        shards,
        mesh=mesh,
        in_specs=(P("gx", "gy", None, None), P(), P(), P()),
        out_specs=(P("gx", "gy", None, None), P(), P()),
        check_vma=False,
    )
```
